32 devices in a mesh: sweep: 2 (over core), cx: 4 (over y, x), cy: 4 (over z).
Axes of the slice: x: 2, y: 2, z: 4, core: 2. Of those that a mesh axis runs over, the one named last changes fastest.
Arguments:
- right_side: bfloat16 [8, 135, 16, 512], P('sweep', None, 'cx', 'cy'), may hold values from -6 to 6
- previous: bfloat16 [8, 135, 16, 512], P('sweep', None, 'cx', 'cy'), may hold values from -6 to 6
- diag_inverse: float32 [4, 135, 135], replicated
- face_blocks: float32 [4, 6, 135, 135], replicated
- pattern: int32 [8], P('sweep'), may hold values from 0 to 3
- live_count: int32 [8, 4, 4], P('sweep', 'cx', 'cy'), may hold values from 384 to 512, as said below
Outputs:
- solution: float32 [8, 135, 16, 512], P('sweep', None, 'cx', 'cy')
The draws below stay inside these ranges and needn't reach their ends.
Inputs may be any that keep to these rules, and one draw needn't show every extreme that they name: In a device's band the slots are numbered i * 128 + j by the device's own cell indices; the first live_count of them hold elements. In every draw some band of some device holds 512 elements.
All inputs are finite; a program needn't handle non-finite values.
Results may differ from the reference program's by a relative error of at most 0.0003.
Values may be sent and summed in bfloat16 or wider, within the bound.
No kernel may reach another device: no remote copies, remote signals or barrier semaphores. Data moves between devices by JAX's collectives and lax.ppermute only.
A program may use at most 64 MiB of HBM per device.

```python
import math
import jax
import jax.numpy as jnp
from jax import lax

NV = 135
PATTERNS = 4
EX = 4
EY = 128
CELLS = 512
Z = 8
X = 16
Y = 512
N_CX = 4
N_CY = 4


def block_tables(key):
    basis_key, mixing_key, rate_key, pick_key, noise_key, face_key = jax.random.split(key, 6)
    shared_matrix = jax.random.normal(basis_key, (NV, NV), jnp.float32)
    own_matrix = jax.random.normal(mixing_key, (PATTERNS, NV, NV), jnp.float32)
    bases = jnp.linalg.qr(shared_matrix[None] + 0.4 * own_matrix)[0]
    slow_total = NV // 2
    ranking = jax.random.permutation(pick_key, NV)
    slow_mask = ranking < slow_total
    slow_key, fast_key = jax.random.split(rate_key)
    slow_rates = jax.random.uniform(slow_key, (PATTERNS, NV), jnp.float32, 0.985, 0.997)
    fast_rates = jax.random.uniform(fast_key, (PATTERNS, NV), jnp.float32, 0.9, 0.96)
    rates = jnp.where(slow_mask[None, :], slow_rates, fast_rates)
    transfer = -jnp.einsum('puk,pk,pvk->puv', bases, rates, bases, precision=lax.Precision.HIGHEST)
    noise = jax.random.normal(noise_key, (PATTERNS, NV, NV), jnp.float32) * (0.3 / math.sqrt(NV))
    identity_block = jnp.eye(NV, dtype=jnp.float32)[None]
    inverse_table = (identity_block + noise) * 0.25
    diagonal_blocks = 4.0 * jnp.linalg.inv(identity_block + noise)
    upstream = jnp.einsum('puv,pvw->puw', diagonal_blocks, transfer, precision=lax.Precision.HIGHEST)
    others = jax.random.normal(face_key, (PATTERNS, 5, NV, NV), jnp.float32) * (0.35 / math.sqrt(NV))
    return (inverse_table, jnp.concatenate([upstream[:, None], others], axis=1))


def draw_diag_inverse(key, part):
    return block_tables(jax.random.fold_in(key, 17))[0]


def draw_face_blocks(key, part):
    return block_tables(jax.random.fold_in(key, 17))[1]


def draw_live_count(key, part):
    count_key, place_key = jax.random.split(jax.random.fold_in(key, 29))
    counts = jax.random.randint(count_key, (Z, N_CX, N_CY), 3 * CELLS // 4, CELLS + 1, jnp.int32)
    full_at = jax.random.randint(place_key, (), 0, Z * N_CX * N_CY, jnp.int32)
    flat_index = jnp.arange(Z * N_CX * N_CY, dtype=jnp.int32).reshape(Z, N_CX, N_CY)
    return jnp.where(flat_index == full_at, CELLS, counts).astype(jnp.int32)


def with_ends(values, rng, smallest, high):
    longest = values.shape.index(max(values.shape))
    spots = []
    for shift in (0, 1):
        where = [jax.random.randint(jax.random.fold_in(rng, axis), (), 0, length) for axis, length in enumerate(values.shape)]
        where[longest] = (where[longest] + shift) % values.shape[longest]
        spots.append(tuple(where))
    return values.at[spots[0]].set(smallest).at[spots[1]].set(high)


def level_of(own_key, extent, shards, smallest, largest):
    level = 1.0
    for axis_at, parts in shards:
        steps = jax.random.uniform(jax.random.fold_in(jax.random.fold_in(own_key, 6), axis_at), (parts,), jnp.float32, smallest / len(shards), largest / len(shards))
        level = level * jnp.repeat(jnp.exp(steps), extent[axis_at] // parts).reshape((-1,) + (1,) * (len(extent) - 1 - axis_at))
    return level


def centred(stream_key, dims, width, reach, pieces=(), held_as=jnp.bfloat16):
    factor_of = level_of(stream_key, dims, pieces, -0.22, 0.18) if pieces else 1.0
    array = jax.random.normal(stream_key, dims, jnp.float32) * width * factor_of
    return jnp.minimum(jnp.maximum(array, -reach), reach).astype(held_as)


def setup_inputs(seed: int = 0) -> dict:
    arg_keys = jax.random.split(jax.random.key(seed), 7)
    return {
        "right_side": centred(arg_keys[0], (Z, NV, X, Y), 1.0, 6.0, ((0, 2), (2, 4), (3, 4))),
        "previous": centred(arg_keys[1], (Z, NV, X, Y), 1.0, 6.0, ((0, 2), (2, 4), (3, 4))),
        "diag_inverse": draw_diag_inverse(jax.random.fold_in(arg_keys[6], 71), 0),
        "face_blocks": draw_face_blocks(jax.random.fold_in(arg_keys[6], 71), 0),
        "pattern": with_ends(jax.random.randint(arg_keys[4], (Z,), 0, PATTERNS), jax.random.fold_in(arg_keys[4], 1), 0, PATTERNS - 1).astype(jnp.int32),
        "live_count": draw_live_count(jax.random.fold_in(arg_keys[6], 71), 0),
    }


full_precision = lax.Precision.HIGHEST

def apply_block(block, neighbour_field):
    return jnp.einsum('uv,vxy->uxy', block, neighbour_field, precision=full_precision)

def reference(right_side, previous, diag_inverse, face_blocks, pattern, live_count):
    band_total = right_side.shape[0]
    row_slot = jnp.arange(X, dtype=jnp.int32) % EX * EY
    col_slot = jnp.arange(Y, dtype=jnp.int32) % EY
    slot_index = row_slot[:, None] + col_slot[None, :]
    owner_x = jnp.arange(X, dtype=jnp.int32) // EX
    owner_y = jnp.arange(Y, dtype=jnp.int32) // EY
    pattern_table = jnp.arange(PATTERNS, dtype=jnp.int32)

    def advance(upstream, band_index):
        selector = (pattern_table == pattern[band_index]).astype(jnp.float32)
        inverse = jnp.einsum('p,puv->uv', selector, diag_inverse, precision=full_precision)
        blocks = jnp.einsum('p,pfuv->fuv', selector, face_blocks, precision=full_precision)
        current = lax.dynamic_index_in_dim(previous, band_index, 0, keepdims=False).astype(jnp.float32)
        next_index = jnp.minimum(band_index + 1, band_total - 1)
        downstream = lax.dynamic_index_in_dim(previous, next_index, 0, keepdims=False).astype(jnp.float32)
        downstream = jnp.where(band_index + 1 < band_total, downstream, jnp.zeros_like(downstream))
        padded = jnp.pad(current, ((0, 0), (1, 1), (1, 1)))
        residual_base = lax.dynamic_index_in_dim(right_side, band_index, 0, keepdims=False).astype(jnp.float32)
        residual_base = residual_base - apply_block(blocks[1], downstream)
        residual_base = residual_base - apply_block(blocks[2], padded[:, :-2, 1:-1])
        residual_base = residual_base - apply_block(blocks[3], padded[:, 2:, 1:-1])
        residual_base = residual_base - apply_block(blocks[4], padded[:, 1:-1, :-2])
        residual_base = residual_base - apply_block(blocks[5], padded[:, 1:-1, 2:])
        residual_base = residual_base - apply_block(blocks[0], upstream)
        counts = lax.dynamic_index_in_dim(live_count, band_index, 0, keepdims=False)
        limits = counts[owner_x][:, owner_y]
        live_mask = (slot_index < limits).astype(jnp.float32)
        updated = live_mask[None] * apply_block(inverse, residual_base)
        return (updated, updated)
    initial = jnp.zeros(right_side.shape[1:], jnp.float32)
    final_carry, solution = lax.scan(advance, initial, jnp.arange(band_total, dtype=jnp.int32))
    return solution
```

```python
import functools

import jax
import jax.numpy as jnp
from jax import lax
from jax.experimental import pallas as pl
from jax.experimental.pallas import tpu as pltpu
from jax.sharding import PartitionSpec as P

F32, BF16 = jnp.float32, jnp.bfloat16
VMEM = pl.BlockSpec(memory_space=pltpu.VMEM)
SMEM = pl.BlockSpec(memory_space=pltpu.SMEM)


def rounded(count, unit):
    return (count + unit - 1) // unit * unit


def padded_rows(count):
    return rounded(count, 16)


def product(left, right):
    return jnp.dot(left, right, preferred_element_type=F32)


def halves(value):
    high = value.astype(BF16)
    return high, (value - high.astype(F32)).astype(BF16)


def store_halves(ref, value):
    count = value.shape[0]
    start = padded_rows(count)
    high, low = halves(value)
    ref[0:count, :] = high
    ref[start : start + count, :] = low


def apply(stacked, right, count):
    both = product(stacked, right)
    start = padded_rows(count)
    return both[0:count] + both[start : start + count]


def apply_halves(stacked, right, count):
    high, low = right
    rest = product(stacked[0 : padded_rows(count)], low)
    return apply(stacked, high, count) + rest[0:count]


def lane_blocks(ref, start, count, across):
    return [ref[pl.ds(start + i, count, stride=across), :] for i in range(across)]


def pack_kernel(bands, count, across, prev, face_even, face_odd, side_even, side_odd, first, wide, rows_even, rows_odd):
    along = prev.shape[-1]
    odd_x = lax.axis_index("cx") % 2 == 1
    odd_y = lax.axis_index("cy") % 2 == 1
    wide[...] = prev[...].astype(F32)
    first[...] = prev[0 : count * across, :]
    row = lax.broadcasted_iota(jnp.int32, (8, along), 0)
    lane = lax.broadcasted_iota(jnp.int32, (8, along), 1)
    last = along - 1
    even_lane, odd_lane = jnp.where(odd_y, 0, last), jnp.where(odd_y, last, 0)
    chosen = jnp.where(row == 0, even_lane, odd_lane)
    pick = jnp.where(lane == chosen, 1.0, 0.0).astype(BF16)
    for z in range(bands):
        blocks = lane_blocks(wide, z * count * across, count, across)
        low, high = blocks[0], blocks[-1]
        face_even[z] = jnp.where(odd_x, low, high).astype(BF16)
        face_odd[z] = jnp.where(odd_x, high, low).astype(BF16)
        for i in range(across):
            found = lax.dot_general(
                pick, blocks[i].astype(BF16), (((1,), (1,)), ((), ())), preferred_element_type=F32
            )
            at = z * across + i
            rows_even[at : at + 1, :] = found[0:1]
            rows_odd[at : at + 1, :] = found[1:2]
    side_even[...] = rows_even[...].astype(BF16)
    side_odd[...] = rows_odd[...].astype(BF16)


def local_kernel(
    bands, count, across, pattern, right, prev, follow, side_even, side_odd, faces, inverses,
    base, reach, across_maps, inverse_maps, step_maps, wide, wide_right, wide_follow, sides, work, reach_work,
):
    along = prev.shape[-1]
    block = count * across
    odd_y = lax.axis_index("cy") % 2 == 1
    has_next = lax.axis_index("sweep") < lax.axis_size("sweep") - 1
    wide[...] = prev[...].astype(F32)
    wide_right[...] = right[...].astype(F32)
    wide_follow[...] = jnp.where(has_next, follow[...].astype(F32), 0.0)
    even, odd = side_even[...].astype(F32), side_odd[...].astype(F32)
    total = bands * across
    sides[0:total, 0:count] = jnp.where(odd_y, even, odd)
    sides[total : 2 * total, 0:count] = jnp.where(odd_y, odd, even)
    columns = sides[...].T
    lane = lax.broadcasted_iota(jnp.int32, (count, along), 1)
    fields = []
    for z in range(bands):
        fields.append(lane_blocks(wide, z * block, count, across))
    fields.append(lane_blocks(wide_follow, 0, count, across))

    def join(blocks):
        return jnp.concatenate(blocks, axis=1).astype(BF16)

    for z in range(bands):
        which = pattern[z]
        mine = fields[z]
        behind, ahead = [], []
        for i in range(across):
            at = z * across + i
            behind.append(
                jnp.where(lane == 0, columns[0:count, at : at + 1], pltpu.roll(mine[i], 1, axis=1))
            )
            at = at + total
            ahead.append(
                jnp.where(
                    lane == along - 1, columns[0:count, at : at + 1], pltpu.roll(mine[i], along - 1, axis=1)
                )
            )
        sums = jnp.concatenate(lane_blocks(wide_right, z * block, count, across), axis=1)
        whole = join(mine)
        for face, field in ((1, join(fields[z + 1])), (4, join(behind)), (5, join(ahead))):
            store_halves(work, faces[face, :, which, :])
            sums = sums - apply(work[...], field, count)
        base[z] = sums
        for place in range(2):
            store_halves(across_maps.at[z, place], faces[2 + place, :, which, :])
        edge = (across - 1) * along
        base[z, :, along:] = base[z, :, along:] - apply(across_maps[z, 0], whole[:, :edge], count)
        base[z, :, :edge] = base[z, :, :edge] - apply(across_maps[z, 1], whole[:, along:], count)
        inverse = inverses[:, which, :]
        store_halves(inverse_maps.at[z], inverse)
        step = -apply_halves(inverse_maps[z], halves(faces[0, :, which, :]), count)
        store_halves(step_maps.at[z], step)
    reach[bands - 1] = inverse_maps[bands - 1]
    reach_work[...] = step_maps[bands - 1]
    start = padded_rows(count)
    for z in range(bands - 2, -1, -1):
        parts = (inverse_maps[z, 0:count, :], inverse_maps[z, start : start + count, :])
        store_halves(reach.at[z], apply_halves(reach_work[...], parts, count))
        if z > 0:
            parts = (step_maps[z, 0:count, :], step_maps[z, start : start + count, :])
            store_halves(reach_work, apply_halves(reach_work[...], parts, count))


def edge_kernel(bands, count, across, live, base, reach, across_maps, face_even, face_odd, last, high, low):
    cells = base.shape[-1]
    along = cells // across
    odd_x = lax.axis_index("cx") % 2 == 1
    slot = lax.broadcasted_iota(jnp.int32, (count, cells), 1)
    edge = cells - along
    shortest = live[bands - 1]
    sums = None
    for z in range(bands - 1, -1, -1):
        even, odd = face_even[z].astype(F32), face_odd[z].astype(F32)
        minus = jnp.where(odd_x, even, odd).astype(BF16)
        plus = jnp.where(odd_x, odd, even).astype(BF16)
        rows = base[z]
        rows = jnp.concatenate(
            [
                rows[:, :along] - apply(across_maps[z, 0], minus, count),
                rows[:, along:edge],
                rows[:, edge:] - apply(across_maps[z, 1], plus, count),
            ],
            axis=1,
        )
        parts = halves(rows)
        high[z], low[z] = parts
        shortest = jnp.minimum(shortest, live[z])
        kept = slot < shortest
        parts = halves(jnp.where(kept, rows, 0.0))
        term = apply_halves(reach[z], parts, count)
        sums = term if sums is None else sums + term
    last[...] = sums


def sweep_kernel(bands, count, live, high, low, inverse_maps, step_maps, states, chains):
    cells = high.shape[-1]
    slot = lax.broadcasted_iota(jnp.int32, (count, cells), 1)
    current = None
    start = padded_rows(count)
    for z in range(bands):
        value = apply_halves(inverse_maps[z], (high[z], low[z]), count)
        if z > 0:
            value = value + apply_halves(step_maps[z], halves(current), count)
        current = jnp.where(slot < live[z], value, 0.0)
        states[z] = current
    chains[0] = step_maps[0]
    for z in range(1, bands):
        parts = (chains[z - 1, 0:count, :], chains[z - 1, start : start + count, :])
        store_halves(chains.at[z], apply_halves(step_maps[z], parts, count))


def finish_kernel(bands, count, across, live, states, chains, incoming, out):
    cells = incoming.shape[-1]
    along = cells // across
    slot = lax.broadcasted_iota(jnp.int32, (count, cells), 1)
    parts = halves(jnp.where(lax.axis_index("sweep") > 0, incoming[...], 0.0))
    shortest = live[0]
    for z in range(bands):
        shortest = jnp.minimum(shortest, live[z])
        moved = apply_halves(chains[z], parts, count)
        value = states[z] + jnp.where(slot < shortest, moved, 0.0)
        for i in range(across):
            out[pl.ds(z * count * across + i, count, stride=across), :] = value[:, i * along : (i + 1) * along]


def call(kernel, out, specs, scratch=(), flops=0, moved=0):
    return pl.pallas_call(
        kernel,
        out_shape=out,
        in_specs=specs,
        out_specs=jax.tree.map(lambda _: VMEM, out),
        scratch_shapes=scratch,
        cost_estimate=pl.CostEstimate(flops=flops, bytes_accessed=moved, transcendentals=0),
        compiler_params=pltpu.CompilerParams(vmem_limit_bytes=40 * 2**20),
    )


def swapped(value, axis, first):
    pairs = []
    for left in range(first, lax.axis_size(axis) - 1, 2):
        pairs += [(left, left + 1), (left + 1, left)]
    return lax.ppermute(value, axis, pairs)


def passed_along(value, axis, steps):
    count = lax.axis_size(axis)
    if count == 2:
        return swapped(value, axis, 0)
    first, last = (max(0, -steps), min(count, count - steps))
    return lax.ppermute(value, axis, [(source, source + steps) for source in range(first, last)])


def on_device(right_side, previous, diag_inverse, face_blocks, pattern, live_count):
    bands, count, across, along = right_side.shape
    cells, rows = across * along, bands * count * across
    pads = 2 * padded_rows(count)
    shape = jax.ShapeDtypeStruct
    right = right_side.reshape(rows, along)
    prev = previous.reshape(rows, along)
    faces = face_blocks.transpose(1, 2, 0, 3)
    inverses = diag_inverse.transpose(1, 0, 2)
    live = live_count.reshape(bands)
    face = shape((bands, count, along), BF16)
    side = shape((bands * across, count), BF16)
    side_rows = pltpu.VMEM((bands * across, count), F32)
    face_even, face_odd, side_even, side_odd, first = call(
        functools.partial(pack_kernel, bands, count, across),
        (face, face, side, side, shape((count * across, along), BF16)),
        [VMEM],
        [pltpu.VMEM((rows, along), F32), side_rows, side_rows],
        moved=rows * along * 4,
    )(prev)
    face_even = swapped(face_even, "cx", 0)
    face_odd = swapped(face_odd, "cx", 1)
    side_even = swapped(side_even, "cy", 0)
    side_odd = swapped(side_odd, "cy", 1)
    follow = passed_along(first, "sweep", -1)
    matrix = shape((bands, pads, count), BF16)
    base, reach, across_maps, inverse_maps, step_maps = call(
        functools.partial(local_kernel, bands, count, across),
        (shape((bands, count, cells), F32), matrix, shape((bands, 2, pads, count), BF16), matrix, matrix),
        [SMEM] + [VMEM] * 7,
        [
            pltpu.VMEM((rows, along), F32),
            pltpu.VMEM((rows, along), F32),
            pltpu.VMEM((count * across, along), F32),
            pltpu.VMEM((rounded(2 * bands * across, 128), rounded(count, 128)), F32),
            pltpu.VMEM((pads, count), BF16),
            pltpu.VMEM((pads, count), BF16),
        ],
        flops=bands * 10 * count * count * cells * 2,
        moved=8 * 2**20,
    )(pattern, right, prev, follow, side_even, side_odd, faces, inverses)
    last, high, low = call(
        functools.partial(edge_kernel, bands, count, across),
        (shape((count, cells), F32), shape((bands, count, cells), BF16), shape((bands, count, cells), BF16)),
        [SMEM] + [VMEM] * 5,
        flops=bands * 5 * count * count * cells * 2,
        moved=4 * 2**20,
    )(live, base, reach, across_maps, face_even, face_odd)
    states, chains = call(
        functools.partial(sweep_kernel, bands, count),
        (shape((bands, count, cells), F32), matrix),
        [SMEM] + [VMEM] * 4,
        flops=bands * 6 * count * count * cells * 2,
        moved=4 * 2**20,
    )(live, high, low, inverse_maps, step_maps)
    incoming = passed_along(last, "sweep", 1)
    if lax.axis_size("sweep") > 2:
        start = padded_rows(count)
        end_map = chains[-1, 0:count].astype(F32) + chains[-1, start : start + count].astype(F32)
        slot = jnp.arange(cells, dtype=jnp.int32)
        kept = (slot < jnp.min(live)).astype(F32)

        def relay(_, arriving):
            product = jnp.dot(end_map, arriving, precision=lax.Precision.HIGHEST)
            return passed_along(last + kept[None, :] * product, "sweep", 1)

        incoming = lax.fori_loop(0, lax.axis_size("sweep") - 2, relay, incoming)
    out = call(
        functools.partial(finish_kernel, bands, count, across),
        shape((rows, along), F32),
        [SMEM] + [VMEM] * 3,
        flops=bands * 3 * count * count * cells * 2,
        moved=3 * 2**20,
    )(live, states, chains, incoming)
    return out.reshape(bands, count, across, along)


def solution(mesh):
    return jax.shard_map(
        on_device,
        mesh=mesh,
        in_specs=(
            P("sweep", None, "cx", "cy"),
            P("sweep", None, "cx", "cy"),
            P(),
            P(),
            P("sweep"),
            P("sweep", "cx", "cy"),
        ),
        out_specs=P("sweep", None, "cx", "cy"),
        check_vma=False,
    )
```

```python
import functools

import jax
import jax.numpy as jnp
from jax import lax
from jax.experimental import pallas as pl
from jax.experimental.pallas import tpu as pltpu
from jax.sharding import PartitionSpec as P

F32, BF16 = jnp.float32, jnp.bfloat16
VMEM = pl.BlockSpec(memory_space=pltpu.VMEM)
HBM = pl.BlockSpec(memory_space=pltpu.HBM)


def rounded(count, unit):
    return (count + unit - 1) // unit * unit


def padded_rows(count):
    return rounded(count, 16)


def product(left, right):
    return jnp.dot(left, right, preferred_element_type=F32)


def halves(value):
    high = value.astype(BF16)
    return high, (value - high.astype(F32)).astype(BF16)


def store_halves(ref, value):
    count = value.shape[0]
    start = padded_rows(count)
    high, low = halves(value)
    ref[0:count, :] = high
    ref[start : start + count, :] = low


def apply(stacked, right, count):
    both = product(stacked, right)
    start = padded_rows(count)
    return both[0:count] + both[start : start + count]


def apply_halves(stacked, right, count):
    high, low = right
    rest = product(stacked[0 : padded_rows(count)], low)
    return apply(stacked, high, count) + rest[0:count]


def lane_blocks(ref, start, count, across):
    return [ref[pl.ds(start + i, count, stride=across), :] for i in range(across)]


def chunks(rows):
    return 2 if rows % 32 == 0 else 1


def start_copies(source, target, sems, first=0):
    rows = source.shape[0]
    size = rows // chunks(rows)
    copies = []
    for at in range(chunks(rows)):
        window = pl.ds(at * size, size)
        copies.append(pltpu.make_async_copy(source.at[window], target.at[window], sems.at[first + at]))
        copies[-1].start()
    return copies


def pack_kernel(
    bands, count, across, prev, kept, face_even, face_odd, side_even, side_odd, first, wide, rows_even, rows_odd, sems
):
    along = prev.shape[-1]
    rows = prev.shape[0]
    copies = start_copies(prev, kept, sems)
    odd_x = lax.axis_index("cx") % 2 == 1
    odd_y = lax.axis_index("cy") % 2 == 1
    row = lax.broadcasted_iota(jnp.int32, (8, along), 0)
    lane = lax.broadcasted_iota(jnp.int32, (8, along), 1)
    last = along - 1
    even_lane, odd_lane = jnp.where(odd_y, 0, last), jnp.where(odd_y, last, 0)
    chosen = jnp.where(row == 0, even_lane, odd_lane)
    pick = jnp.where(lane == chosen, 1.0, 0.0).astype(BF16)
    size = rows // len(copies)
    done = 0
    for z in range(bands):
        while done * size < (z + 1) * count * across:
            copies[done].wait()
            window = pl.ds(done * size, size)
            wide[window, :] = kept[window, :].astype(F32)
            done += 1
        blocks = lane_blocks(wide, z * count * across, count, across)
        low, high = blocks[0], blocks[-1]
        face_even[z] = jnp.where(odd_x, low, high).astype(BF16)
        face_odd[z] = jnp.where(odd_x, high, low).astype(BF16)
        for i in range(across):
            found = lax.dot_general(
                pick, blocks[i].astype(BF16), (((1,), (1,)), ((), ())), preferred_element_type=F32
            )
            at = z * across + i
            rows_even[at : at + 1, :] = found[0:1]
            rows_odd[at : at + 1, :] = found[1:2]
    first[...] = kept[0 : count * across, :]
    side_even[...] = rows_even[...].astype(BF16)
    side_odd[...] = rows_odd[...].astype(BF16)


def parts(ref, count):
    start = padded_rows(count)
    return ref[0:count, :], ref[start : start + count, :]


def combine(out, left, right, count):
    store_halves(out, apply_halves(left[...], parts(right, count), count))


def matrix_kernel(
    bands, count, pattern_far, live_far, faces, inverses, right,
    right_kept, maps, inverse_maps, step_maps, reach, edge_reach, chains, masks,
    faces_here, inverses_here, pool, pattern, live, sems,
):
    cells = masks.shape[-1]
    copies = [pltpu.make_async_copy(inverses, inverses_here, sems.at[0])]
    order = (0, 2, 3, 1, 4, 5)
    for face in order:
        copies.append(pltpu.make_async_copy(faces.at[face], faces_here.at[face], sems.at[1 + face]))
    copies.append(pltpu.make_async_copy(right, right_kept, sems.at[7]))
    small = [
        pltpu.make_async_copy(pattern_far, pattern, sems.at[8]),
        pltpu.make_async_copy(live_far, live, sems.at[9]),
    ]
    for copy in small + copies:
        copy.start()
    for copy in small:
        copy.wait()
    slot = lax.broadcasted_iota(jnp.int32, (1, cells), 1)
    counts = [live[z] for z in range(bands)]
    before, after = counts[0], counts[bands - 1]
    for z in range(bands):
        before = jnp.minimum(before, counts[z])
        after = jnp.minimum(after, counts[bands - 1 - z])
        for row, limit in ((z, counts[z]), (2 * bands - 1 - z, after), (2 * bands + z, before)):
            masks[row : row + 1, :] = jnp.where(slot < limit, 1.0, 0.0)
    which = [pattern[z] for z in range(bands)]
    copies[0].wait()
    for z in range(bands):
        store_halves(inverse_maps.at[z], inverses_here[:, which[z], :])
    copies[1].wait()
    for z in range(bands):
        upstream = halves(faces_here[0, :, which[z], :])
        store_halves(step_maps.at[z], -apply_halves(inverse_maps[z], upstream, count))
    spare = [0]

    def fresh():
        spare[0] += 1
        return pool.at[spare[0] - 1]

    def solve(low, high, top):
        if high - low == 1:
            return {low: inverse_maps.at[low]}, step_maps.at[low]
        middle = (low + high) // 2
        near, near_step = solve(low, middle, False)
        found, far_step = solve(middle, high, False)
        for z, ref in near.items():
            target = reach.at[z] if top else fresh()
            combine(target, far_step, ref, count)
            found[z] = target
        step = None
        if not top:
            step = fresh()
            combine(step, far_step, near_step, count)
        if top:
            for z in range(middle, high):
                reach[z] = found[z][...]
        return found, step

    solve(0, bands, True)
    for place, face in enumerate(order[1:]):
        copies[2 + place].wait()
        for z in range(bands):
            ref = maps.at[z, face - 1]
            store_halves(ref, faces_here[face, :, which[z], :])
            if place < 2:
                combine(edge_reach.at[z, place], reach.at[z], ref, count)
    chains[0] = step_maps[0]
    for z in range(1, bands):
        combine(chains.at[z], step_maps.at[z], chains.at[z - 1], count)
    copies[-1].wait()


def local_kernel(
    bands, count, across, right, prev, follow, side_even, side_odd, maps, reach, masks,
    base, partial, wide, wide_right, wide_follow, sides,
):
    along = prev.shape[-1]
    block = count * across
    odd_y = lax.axis_index("cy") % 2 == 1
    has_next = lax.axis_index("sweep") < lax.axis_size("sweep") - 1
    wide[...] = prev[...].astype(F32)
    wide_right[...] = right[...].astype(F32)
    wide_follow[...] = jnp.where(has_next, follow[...].astype(F32), 0.0)
    even, odd = side_even[...].astype(F32), side_odd[...].astype(F32)
    total = bands * across
    sides[0:total, 0:count] = jnp.where(odd_y, even, odd)
    sides[total : 2 * total, 0:count] = jnp.where(odd_y, odd, even)
    columns = sides[...].T
    lane = lax.broadcasted_iota(jnp.int32, (count, along), 1)
    fields = []
    for z in range(bands):
        fields.append(lane_blocks(wide, z * block, count, across))
    fields.append(lane_blocks(wide_follow, 0, count, across))

    def join(blocks):
        return jnp.concatenate(blocks, axis=1).astype(BF16)

    edge = (across - 1) * along
    sums = None
    for z in range(bands):
        mine = fields[z]
        behind, ahead = [], []
        for i in range(across):
            at = z * across + i
            column = columns[0:count, at : at + 1]
            behind.append(jnp.where(lane == 0, column, pltpu.roll(mine[i], 1, axis=1)))
            column = columns[0:count, at + total : at + total + 1]
            ahead.append(jnp.where(lane == along - 1, column, pltpu.roll(mine[i], along - 1, axis=1)))
        whole = join(mine)
        full = apply(maps[z, 0], join(fields[z + 1]), count)
        full = full + apply(maps[z, 3], join(behind), count)
        full = full + apply(maps[z, 4], join(ahead), count)
        minus = apply(maps[z, 1], whole[:, :edge], count)
        plus = apply(maps[z, 2], whole[:, along:], count)
        own = lane_blocks(wide_right, z * block, count, across)
        rows = []
        for i in range(across):
            value = own[i] - full[:, i * along : (i + 1) * along]
            if i > 0:
                value = value - minus[:, (i - 1) * along : i * along]
            if i < across - 1:
                value = value - plus[:, i * along : (i + 1) * along]
            rows.append(value)
        rows = jnp.concatenate(rows, axis=1)
        base[z] = rows
        term = apply_halves(reach[z], halves(rows * masks[bands + z : bands + z + 1, :]), count)
        sums = term if sums is None else sums + term
    partial[...] = sums


def edges_of(face_even, face_odd, z):
    odd_x = lax.axis_index("cx") % 2 == 1
    even, odd = face_even[z].astype(F32), face_odd[z].astype(F32)
    return jnp.where(odd_x, even, odd), jnp.where(odd_x, odd, even)


def edge_kernel(bands, count, across, partial, edge_reach, masks, face_even, face_odd, last):
    cells = partial.shape[-1]
    along = cells // across
    edge = cells - along
    first, final = partial[:, :along], partial[:, edge:]
    for z in range(bands):
        minus, plus = edges_of(face_even, face_odd, z)
        mask = masks[bands + z : bands + z + 1, :]
        first = first - apply(edge_reach[z, 0], (minus * mask[:, :along]).astype(BF16), count)
        final = final - apply(edge_reach[z, 1], (plus * mask[:, edge:]).astype(BF16), count)
    last[:, :along] = first
    last[:, along:edge] = partial[:, along:edge]
    last[:, edge:] = final


def sweep_kernel(bands, count, across, base, masks, maps, inverse_maps, step_maps, face_even, face_odd, states):
    cells = base.shape[-1]
    along = cells // across
    edge = cells - along
    shares = []
    for z in range(bands):
        minus, plus = edges_of(face_even, face_odd, z)
        rows = base[z]
        rows = jnp.concatenate(
            [
                rows[:, :along] - apply(maps[z, 1], minus.astype(BF16), count),
                rows[:, along:edge],
                rows[:, edge:] - apply(maps[z, 2], plus.astype(BF16), count),
            ],
            axis=1,
        )
        shares.append(apply_halves(inverse_maps[z], halves(rows), count))
    current = None
    for z in range(bands):
        value = shares[z]
        if z > 0:
            value = value + apply_halves(step_maps[z], halves(current), count)
        current = value * masks[z : z + 1, :]
        states[z] = current


def finish_kernel(bands, count, across, masks, states, chains, incoming, out, staged, sems):
    cells = incoming.shape[-1]
    along = cells // across
    rows = staged.shape[0]
    right = halves(jnp.where(lax.axis_index("sweep") > 0, incoming[...], 0.0))
    size = rows // chunks(rows)
    copies = []
    for z in range(bands):
        moved = apply_halves(chains[z], right, count)
        value = states[z] + moved * masks[2 * bands + z : 2 * bands + z + 1, :]
        for i in range(across):
            staged[pl.ds(z * count * across + i, count, stride=across), :] = value[:, i * along : (i + 1) * along]
        while (len(copies) + 1) * size <= (z + 1) * count * across:
            at = len(copies)
            window = pl.ds(at * size, size)
            copies.append(pltpu.make_async_copy(staged.at[window], out.at[window], sems.at[at]))
            copies[-1].start()
    for copy in copies:
        copy.wait()


def call(kernel, out, specs, scratch=(), flops=0, moved=0, out_specs=None):
    return pl.pallas_call(
        kernel,
        out_shape=out,
        in_specs=specs,
        out_specs=out_specs or jax.tree.map(lambda _: VMEM, out),
        scratch_shapes=scratch,
        cost_estimate=pl.CostEstimate(flops=flops, bytes_accessed=moved, transcendentals=0),
        compiler_params=pltpu.CompilerParams(vmem_limit_bytes=32 * 2**20),
    )


def in_hbm(value):
    return pltpu.with_memory_space_constraint(value, pltpu.HBM)


def swapped(value, axis, first):
    pairs = []
    for left in range(first, lax.axis_size(axis) - 1, 2):
        pairs += [(left, left + 1), (left + 1, left)]
    return lax.ppermute(value, axis, pairs)


def passed_along(value, axis, steps):
    count = lax.axis_size(axis)
    if count == 2:
        return swapped(value, axis, 0)
    first, last = (max(0, -steps), min(count, count - steps))
    return lax.ppermute(value, axis, [(source, source + steps) for source in range(first, last)])


def on_device(right_side, previous, diag_inverse, face_blocks, pattern, live_count):
    bands, count, across, along = right_side.shape
    cells, rows = across * along, bands * count * across
    pads = 2 * padded_rows(count)
    shape = jax.ShapeDtypeStruct
    right = in_hbm(right_side.reshape(rows, along))
    prev = in_hbm(previous.reshape(rows, along))
    faces = in_hbm(face_blocks.transpose(1, 2, 0, 3))
    inverses = in_hbm(diag_inverse.transpose(1, 0, 2))
    live = in_hbm(live_count.reshape(bands))
    pattern = in_hbm(pattern)
    face = shape((bands, count, along), BF16)
    side = shape((bands * across, count), BF16)
    field = shape((rows, along), BF16)
    side_rows = pltpu.VMEM((bands * across, count), F32)
    wide = pltpu.VMEM((rows, along), F32)
    kept, face_even, face_odd, side_even, side_odd, first = call(
        functools.partial(pack_kernel, bands, count, across),
        (field, face, face, side, side, shape((count * across, along), BF16)),
        [HBM],
        [wide, side_rows, side_rows, pltpu.SemaphoreType.DMA((2,))],
        moved=rows * along * 4,
    )(prev)
    face_even = swapped(face_even, "cx", 0)
    face_odd = swapped(face_odd, "cx", 1)
    side_even = swapped(side_even, "cy", 0)
    side_odd = swapped(side_odd, "cy", 1)
    follow = passed_along(first, "sweep", -1)
    matrix = shape((bands, pads, count), BF16)
    step_flops = count * count * cells * 2
    right_kept, maps, inverse_maps, step_maps, reach, edge_reach, chains, masks = call(
        functools.partial(matrix_kernel, bands, count),
        (
            field,
            shape((bands, 5, pads, count), BF16),
            matrix,
            matrix,
            matrix,
            shape((bands, 2, pads, count), BF16),
            matrix,
            shape((3 * bands, cells), F32),
        ),
        [HBM] * 5,
        [
            pltpu.VMEM(faces.shape, F32),
            pltpu.VMEM(inverses.shape, F32),
            pltpu.VMEM((4 * bands, pads, count), BF16),
            pltpu.SMEM((bands,), jnp.int32),
            pltpu.SMEM((bands,), jnp.int32),
            pltpu.SemaphoreType.DMA((10,)),
        ],
        flops=bands * 5 * step_flops,
        moved=4 * 2**20,
    )(pattern, live, faces, inverses, right)
    base, partial = call(
        functools.partial(local_kernel, bands, count, across),
        (shape((bands, count, cells), F32), shape((count, cells), F32)),
        [VMEM] * 8,
        [
            wide,
            wide,
            pltpu.VMEM((count * across, along), F32),
            pltpu.VMEM((rounded(2 * bands * across, 128), rounded(count, 128)), F32),
        ],
        flops=bands * 13 * step_flops,
        moved=2**20,
    )(right_kept, kept, follow, side_even, side_odd, maps, reach, masks)
    last = call(
        functools.partial(edge_kernel, bands, count, across),
        shape((count, cells), F32),
        [VMEM] * 5,
        flops=bands * step_flops,
        moved=2**20,
    )(partial, edge_reach, masks, face_even, face_odd)
    states = call(
        functools.partial(sweep_kernel, bands, count, across),
        shape((bands, count, cells), F32),
        [VMEM] * 7,
        flops=bands * 7 * step_flops,
        moved=2**20,
    )(base, masks, maps, inverse_maps, step_maps, face_even, face_odd)
    incoming = passed_along(last, "sweep", 1)
    if lax.axis_size("sweep") > 2:
        start = padded_rows(count)
        end_map = chains[-1, 0:count].astype(F32) + chains[-1, start : start + count].astype(F32)
        slot = jnp.arange(cells, dtype=jnp.int32)
        kept = (slot < jnp.min(live_count)).astype(F32)

        def relay(_, arriving):
            product = jnp.dot(end_map, arriving, precision=lax.Precision.HIGHEST)
            return passed_along(last + kept[None, :] * product, "sweep", 1)

        incoming = lax.fori_loop(0, lax.axis_size("sweep") - 2, relay, incoming)
    out = call(
        functools.partial(finish_kernel, bands, count, across),
        shape((rows, along), F32),
        [VMEM] * 4,
        [wide, pltpu.SemaphoreType.DMA((2,))],
        flops=bands * 3 * step_flops,
        moved=2**20,
        out_specs=HBM,
    )(masks, states, chains, incoming)
    return out.reshape(bands, count, across, along)


def solution(mesh):
    return jax.shard_map(
        on_device,
        mesh=mesh,
        in_specs=(
            P("sweep", None, "cx", "cy"),
            P("sweep", None, "cx", "cy"),
            P(),
            P(),
            P("sweep"),
            P("sweep", "cx", "cy"),
        ),
        out_specs=P("sweep", None, "cx", "cy"),
        check_vma=False,
    )
```

```python
import functools

import jax
import jax.numpy as jnp
from jax import lax
from jax.experimental import pallas as pl
from jax.experimental.pallas import tpu as pltpu
from jax.sharding import PartitionSpec as P

F32, BF16 = jnp.float32, jnp.bfloat16
VMEM = pl.BlockSpec(memory_space=pltpu.VMEM)
HBM = pl.BlockSpec(memory_space=pltpu.HBM)


def rounded(count, unit):
    return (count + unit - 1) // unit * unit


def padded_rows(count):
    return rounded(count, 16)


def product(left, right):
    return jnp.dot(left, right, preferred_element_type=F32)


def halves(value):
    high = value.astype(BF16)
    return high, (value - high.astype(F32)).astype(BF16)


def store_halves(ref, value):
    high, low = halves(value)
    start = value.shape[0]
    ref[0:start, :] = high
    ref[start : 2 * start, :] = low


def apply(stacked, right, rows):
    both = product(stacked[:, : right.shape[0]], right)
    start = stacked.shape[0] // 2
    return both[0:rows] + both[start : start + rows]


def apply_halves(stacked, right, rows):
    high, low = right
    start = stacked.shape[0] // 2
    rest = product(stacked[0:start, : low.shape[0]], low)
    return apply(stacked, high, rows) + rest[0:rows]


def lane_blocks(ref, start, count, across):
    return [ref[pl.ds(start + i, count, stride=across), :] for i in range(across)]


def chunks(rows):
    return 2 if rows % 32 == 0 else 1


def start_copies(source, target, sems, first=0):
    rows = source.shape[0]
    size = rows // chunks(rows)
    copies = []
    for at in range(chunks(rows)):
        window = pl.ds(at * size, size)
        copies.append(pltpu.make_async_copy(source.at[window], target.at[window], sems.at[first + at]))
        copies[-1].start()
    return copies


def pack_kernel(
    bands, count, across, prev, kept, face_even, face_odd, side_even, side_odd, first, wide, rows_even, rows_odd, sems
):
    along = prev.shape[-1]
    rows = prev.shape[0]
    copies = start_copies(prev, kept, sems)
    odd_x = lax.axis_index("cx") % 2 == 1
    odd_y = lax.axis_index("cy") % 2 == 1
    row = lax.broadcasted_iota(jnp.int32, (8, along), 0)
    lane = lax.broadcasted_iota(jnp.int32, (8, along), 1)
    last = along - 1
    even_lane, odd_lane = jnp.where(odd_y, 0, last), jnp.where(odd_y, last, 0)
    chosen = jnp.where(row == 0, even_lane, odd_lane)
    pick = jnp.where(lane == chosen, 1.0, 0.0).astype(BF16)
    size = rows // len(copies)
    done = 0
    for z in range(bands):
        while done * size < (z + 1) * count * across:
            copies[done].wait()
            window = pl.ds(done * size, size)
            wide[window, :] = kept[window, :].astype(F32)
            done += 1
        blocks = lane_blocks(wide, z * count * across, count, across)
        low, high = blocks[0], blocks[-1]
        face_even[z] = jnp.where(odd_x, low, high).astype(BF16)
        face_odd[z] = jnp.where(odd_x, high, low).astype(BF16)
        for i in range(across):
            found = lax.dot_general(
                pick, blocks[i].astype(BF16), (((1,), (1,)), ((), ())), preferred_element_type=F32
            )
            at = z * across + i
            rows_even[at : at + 1, :] = found[0:1]
            rows_odd[at : at + 1, :] = found[1:2]
    first[...] = kept[0 : count * across, :]
    side_even[...] = rows_even[...].astype(BF16)
    side_odd[...] = rows_odd[...].astype(BF16)


def parts(ref, count):
    start = ref.shape[0] // 2
    return ref[0:count, :], ref[start : start + count, :]


def combine(out, left, right, count):
    store_halves(out, apply_halves(left[...], parts(right, count), out.shape[0] // 2))


def matrix_kernel(
    bands, count, pattern_far, live_far, faces, inverses, right,
    right_kept, maps, inverse_maps, step_maps, reach, edge_reach, chains, masks,
    faces_here, inverses_here, pool, staged, pattern, live, sems,
):
    cells = masks.shape[-1]
    copies = [pltpu.make_async_copy(inverses, inverses_here, sems.at[0])]
    order = (0, 2, 3, 1, 4, 5)
    for face in order:
        copies.append(pltpu.make_async_copy(faces.at[face], faces_here.at[face], sems.at[1 + face]))
    copies.append(pltpu.make_async_copy(right, right_kept, sems.at[7]))
    small = [
        pltpu.make_async_copy(pattern_far, pattern, sems.at[8]),
        pltpu.make_async_copy(live_far, live, sems.at[9]),
    ]
    for copy in small + copies:
        copy.start()
    for copy in small:
        copy.wait()
    staged[...] = jnp.zeros(staged.shape, F32)
    taken = [0]

    def selected(source, band):
        ref = staged.at[taken[0]]
        taken[0] += 1
        ref[0:count, 0:count] = source[:, which[band], :]
        return ref[...]

    slot = lax.broadcasted_iota(jnp.int32, (1, cells), 1)
    counts = [live[z] for z in range(bands)]
    before, after = counts[0], counts[bands - 1]
    for z in range(bands):
        before = jnp.minimum(before, counts[z])
        after = jnp.minimum(after, counts[bands - 1 - z])
        for row, limit in ((z, counts[z]), (2 * bands - 1 - z, after), (2 * bands + z, before)):
            masks[row : row + 1, :] = jnp.where(slot < limit, 1.0, 0.0)
    which = [pattern[z] for z in range(bands)]
    copies[0].wait()
    for z in range(bands):
        store_halves(inverse_maps.at[z], selected(inverses_here, z))
    copies[1].wait()
    for z in range(bands):
        high, low = halves(selected(faces_here.at[0], z))
        upstream = high[0:count], low[0:count]
        store_halves(step_maps.at[z], -apply_halves(inverse_maps[z], upstream, high.shape[0]))
    spare = [0]

    def fresh():
        spare[0] += 1
        return pool.at[spare[0] - 1]

    def solve(low, high, top):
        if high - low == 1:
            return {low: inverse_maps.at[low]}, step_maps.at[low]
        middle = (low + high) // 2
        near, near_step = solve(low, middle, False)
        found, far_step = solve(middle, high, False)
        for z, ref in near.items():
            target = reach.at[z] if top else fresh()
            combine(target, far_step, ref, count)
            found[z] = target
        step = None
        if not top:
            step = fresh()
            combine(step, far_step, near_step, count)
        if top:
            for z in range(middle, high):
                reach[z] = found[z][...]
        return found, step

    solve(0, bands, True)
    for place, face in enumerate(order[1:]):
        copies[2 + place].wait()
        for z in range(bands):
            ref = maps.at[z, face - 1]
            store_halves(ref, selected(faces_here.at[face], z))
            if place < 2:
                combine(edge_reach.at[z, place], reach.at[z], ref, count)
    chains[0] = step_maps[0]
    for z in range(1, bands):
        combine(chains.at[z], step_maps.at[z], chains.at[z - 1], count)
    copies[-1].wait()


def local_kernel(
    bands, count, across, right, prev, follow, side_even, side_odd, maps, reach, masks,
    base, partial, wide, wide_right, wide_follow, sides,
):
    along = prev.shape[-1]
    block = count * across
    odd_y = lax.axis_index("cy") % 2 == 1
    has_next = lax.axis_index("sweep") < lax.axis_size("sweep") - 1
    wide[...] = prev[...].astype(F32)
    wide_right[...] = right[...].astype(F32)
    wide_follow[...] = jnp.where(has_next, follow[...].astype(F32), 0.0)
    even, odd = side_even[...].astype(F32), side_odd[...].astype(F32)
    total = bands * across
    sides[0:total, 0:count] = jnp.where(odd_y, even, odd)
    sides[total : 2 * total, 0:count] = jnp.where(odd_y, odd, even)
    columns = sides[...].T
    lane = lax.broadcasted_iota(jnp.int32, (count, along), 1)
    fields = []
    for z in range(bands):
        fields.append(lane_blocks(wide, z * block, count, across))
    fields.append(lane_blocks(wide_follow, 0, count, across))

    def join(blocks):
        return jnp.concatenate(blocks, axis=1).astype(BF16)

    edge = (across - 1) * along
    sums = None
    for z in range(bands):
        mine = fields[z]
        behind, ahead = [], []
        for i in range(across):
            at = z * across + i
            column = columns[0:count, at : at + 1]
            behind.append(jnp.where(lane == 0, column, pltpu.roll(mine[i], 1, axis=1)))
            column = columns[0:count, at + total : at + total + 1]
            ahead.append(jnp.where(lane == along - 1, column, pltpu.roll(mine[i], along - 1, axis=1)))
        whole = join(mine)
        full = apply(maps[z, 0], join(fields[z + 1]), count)
        full = full + apply(maps[z, 3], join(behind), count)
        full = full + apply(maps[z, 4], join(ahead), count)
        minus = apply(maps[z, 1], whole[:, :edge], count)
        plus = apply(maps[z, 2], whole[:, along:], count)
        own = lane_blocks(wide_right, z * block, count, across)
        rows = []
        for i in range(across):
            value = own[i] - full[:, i * along : (i + 1) * along]
            if i > 0:
                value = value - minus[:, (i - 1) * along : i * along]
            if i < across - 1:
                value = value - plus[:, i * along : (i + 1) * along]
            rows.append(value)
        rows = jnp.concatenate(rows, axis=1)
        base[z] = rows
        term = apply_halves(reach[z], halves(rows * masks[bands + z : bands + z + 1, :]), count)
        sums = term if sums is None else sums + term
    partial[...] = sums


def edges_of(face_even, face_odd, z):
    odd_x = lax.axis_index("cx") % 2 == 1
    even, odd = face_even[z].astype(F32), face_odd[z].astype(F32)
    return jnp.where(odd_x, even, odd), jnp.where(odd_x, odd, even)


def edge_kernel(bands, count, across, partial, edge_reach, masks, face_even, face_odd, last):
    cells = partial.shape[-1]
    along = cells // across
    edge = cells - along
    first, final = partial[:, :along], partial[:, edge:]
    for z in range(bands):
        minus, plus = edges_of(face_even, face_odd, z)
        mask = masks[bands + z : bands + z + 1, :]
        first = first - apply(edge_reach[z, 0], (minus * mask[:, :along]).astype(BF16), count)
        final = final - apply(edge_reach[z, 1], (plus * mask[:, edge:]).astype(BF16), count)
    last[:, :along] = first
    last[:, along:edge] = partial[:, along:edge]
    last[:, edge:] = final


def sweep_kernel(bands, count, across, base, masks, maps, inverse_maps, step_maps, face_even, face_odd, states):
    cells = base.shape[-1]
    along = cells // across
    edge = cells - along
    shares = []
    for z in range(bands):
        minus, plus = edges_of(face_even, face_odd, z)
        rows = base[z]
        rows = jnp.concatenate(
            [
                rows[:, :along] - apply(maps[z, 1], minus.astype(BF16), count),
                rows[:, along:edge],
                rows[:, edge:] - apply(maps[z, 2], plus.astype(BF16), count),
            ],
            axis=1,
        )
        shares.append(apply_halves(inverse_maps[z], halves(rows), count))
    current = None
    for z in range(bands):
        value = shares[z]
        if z > 0:
            value = value + apply_halves(step_maps[z], halves(current), count)
        current = value * masks[z : z + 1, :]
        states[z] = current


def finish_kernel(bands, count, across, masks, states, chains, incoming, out, staged, sems):
    cells = incoming.shape[-1]
    along = cells // across
    rows = staged.shape[0]
    right = halves(jnp.where(lax.axis_index("sweep") > 0, incoming[...], 0.0))
    size = rows // chunks(rows)
    copies = []
    for z in range(bands):
        moved = apply_halves(chains[z], right, count)
        value = states[z] + moved * masks[2 * bands + z : 2 * bands + z + 1, :]
        for i in range(across):
            staged[pl.ds(z * count * across + i, count, stride=across), :] = value[:, i * along : (i + 1) * along]
        while (len(copies) + 1) * size <= (z + 1) * count * across:
            at = len(copies)
            window = pl.ds(at * size, size)
            copies.append(pltpu.make_async_copy(staged.at[window], out.at[window], sems.at[at]))
            copies[-1].start()
    for copy in copies:
        copy.wait()


def call(kernel, out, specs, scratch=(), flops=0, moved=0, out_specs=None):
    return pl.pallas_call(
        kernel,
        out_shape=out,
        in_specs=specs,
        out_specs=out_specs or jax.tree.map(lambda _: VMEM, out),
        scratch_shapes=scratch,
        cost_estimate=pl.CostEstimate(flops=flops, bytes_accessed=moved, transcendentals=0),
        compiler_params=pltpu.CompilerParams(vmem_limit_bytes=32 * 2**20),
    )


def in_hbm(value):
    return pltpu.with_memory_space_constraint(value, pltpu.HBM)


def swapped(value, axis, first):
    pairs = []
    for left in range(first, lax.axis_size(axis) - 1, 2):
        pairs += [(left, left + 1), (left + 1, left)]
    return lax.ppermute(value, axis, pairs)


def passed_along(value, axis, steps):
    count = lax.axis_size(axis)
    if count == 2:
        return swapped(value, axis, 0)
    first, last = (max(0, -steps), min(count, count - steps))
    return lax.ppermute(value, axis, [(source, source + steps) for source in range(first, last)])


def on_device(right_side, previous, diag_inverse, face_blocks, pattern, live_count):
    bands, count, across, along = right_side.shape
    cells, rows = across * along, bands * count * across
    pads, wide_count = 2 * padded_rows(count), rounded(count, 128)
    shape = jax.ShapeDtypeStruct
    right = in_hbm(right_side.reshape(rows, along))
    prev = in_hbm(previous.reshape(rows, along))
    faces = in_hbm(face_blocks.transpose(1, 2, 0, 3))
    inverses = in_hbm(diag_inverse.transpose(1, 0, 2))
    live = in_hbm(live_count.reshape(bands))
    pattern = in_hbm(pattern)
    face = shape((bands, count, along), BF16)
    side = shape((bands * across, count), BF16)
    field = shape((rows, along), BF16)
    side_rows = pltpu.VMEM((bands * across, count), F32)
    wide = pltpu.VMEM((rows, along), F32)
    kept, face_even, face_odd, side_even, side_odd, first = call(
        functools.partial(pack_kernel, bands, count, across),
        (field, face, face, side, side, shape((count * across, along), BF16)),
        [HBM],
        [wide, side_rows, side_rows, pltpu.SemaphoreType.DMA((2,))],
        moved=rows * along * 4,
    )(prev)
    face_even = swapped(face_even, "cx", 0)
    face_odd = swapped(face_odd, "cx", 1)
    side_even = swapped(side_even, "cy", 0)
    side_odd = swapped(side_odd, "cy", 1)
    follow = passed_along(first, "sweep", -1)
    matrix = shape((bands, pads, wide_count), BF16)
    step_flops = count * count * cells * 2
    right_kept, maps, inverse_maps, step_maps, reach, edge_reach, chains, masks = call(
        functools.partial(matrix_kernel, bands, count),
        (
            field,
            shape((bands, 5, pads, wide_count), BF16),
            matrix,
            matrix,
            matrix,
            shape((bands, 2, pads, wide_count), BF16),
            matrix,
            shape((3 * bands, cells), F32),
        ),
        [HBM] * 5,
        [
            pltpu.VMEM(faces.shape, F32),
            pltpu.VMEM(inverses.shape, F32),
            pltpu.VMEM((4 * bands, pads, wide_count), BF16),
            pltpu.VMEM((7 * bands, pads // 2, wide_count), F32),
            pltpu.SMEM((bands,), jnp.int32),
            pltpu.SMEM((bands,), jnp.int32),
            pltpu.SemaphoreType.DMA((10,)),
        ],
        flops=bands * 5 * step_flops,
        moved=4 * 2**20,
    )(pattern, live, faces, inverses, right)
    base, partial = call(
        functools.partial(local_kernel, bands, count, across),
        (shape((bands, count, cells), F32), shape((count, cells), F32)),
        [VMEM] * 8,
        [
            wide,
            wide,
            pltpu.VMEM((count * across, along), F32),
            pltpu.VMEM((rounded(2 * bands * across, 128), rounded(count, 128)), F32),
        ],
        flops=bands * 13 * step_flops,
        moved=2**20,
    )(right_kept, kept, follow, side_even, side_odd, maps, reach, masks)
    last = call(
        functools.partial(edge_kernel, bands, count, across),
        shape((count, cells), F32),
        [VMEM] * 5,
        flops=bands * step_flops,
        moved=2**20,
    )(partial, edge_reach, masks, face_even, face_odd)
    states = call(
        functools.partial(sweep_kernel, bands, count, across),
        shape((bands, count, cells), F32),
        [VMEM] * 7,
        flops=bands * 7 * step_flops,
        moved=2**20,
    )(base, masks, maps, inverse_maps, step_maps, face_even, face_odd)
    incoming = passed_along(last, "sweep", 1)
    if lax.axis_size("sweep") > 2:
        start = padded_rows(count)
        end_map = chains[-1, 0:count, 0:count].astype(F32) + chains[-1, start : start + count, 0:count].astype(F32)
        slot = jnp.arange(cells, dtype=jnp.int32)
        kept = (slot < jnp.min(live_count)).astype(F32)

        def relay(_, arriving):
            product = jnp.dot(end_map, arriving, precision=lax.Precision.HIGHEST)
            return passed_along(last + kept[None, :] * product, "sweep", 1)

        incoming = lax.fori_loop(0, lax.axis_size("sweep") - 2, relay, incoming)
    out = call(
        functools.partial(finish_kernel, bands, count, across),
        shape((rows, along), F32),
        [VMEM] * 4,
        [wide, pltpu.SemaphoreType.DMA((2,))],
        flops=bands * 3 * step_flops,
        moved=2**20,
        out_specs=HBM,
    )(masks, states, chains, incoming)
    return out.reshape(bands, count, across, along)


def solution(mesh):
    return jax.shard_map(
        on_device,
        mesh=mesh,
        in_specs=(
            P("sweep", None, "cx", "cy"),
            P("sweep", None, "cx", "cy"),
            P(),
            P(),
            P("sweep"),
            P("sweep", "cx", "cy"),
        ),
        out_specs=P("sweep", None, "cx", "cy"),
        check_vma=False,
    )
```

```python
import functools

import jax
import jax.numpy as jnp
from jax import lax
from jax.experimental import pallas as pl
from jax.experimental.pallas import tpu as pltpu
from jax.sharding import PartitionSpec as P


F32, BF16 = jnp.float32, jnp.bfloat16
VMEM = pl.BlockSpec(memory_space=pltpu.VMEM)
HBM = pl.BlockSpec(memory_space=pltpu.HBM)


def rounded(count, unit):
    return (count + unit - 1) // unit * unit


def padded_rows(count):
    return rounded(count, 16)


def product(left, right):
    return jnp.dot(left, right, preferred_element_type=F32)


def halves(value):
    high = value.astype(BF16)
    return high, (value - high.astype(F32)).astype(BF16)


def store_halves(ref, value):
    high, low = halves(value)
    start = value.shape[0]
    ref[0:start, :] = high
    ref[start : 2 * start, :] = low


def apply(stacked, right, rows):
    both = product(stacked[:, : right.shape[0]], right)
    start = stacked.shape[0] // 2
    return both[0:rows] + both[start : start + rows]


def apply_halves(stacked, right, rows):
    high, low = right
    start = stacked.shape[0] // 2
    rest = product(stacked[0:start, : low.shape[0]], low)
    return apply(stacked, high, rows) + rest[0:rows]


def lane_blocks(ref, start, count, across):
    return [ref[pl.ds(start + i, count, stride=across), :] for i in range(across)]


def rest_rows(count):
    return rounded(count, 8)


def rest_of(value, head, count):
    piece = value[head:]
    row = lax.broadcasted_iota(jnp.int32, piece.shape, 0)
    return jnp.where(row < count - head, piece, 0.0)


def stacked_rests(pieces, head):
    used = sum(piece.shape[0] for piece in pieces)
    return jnp.concatenate(list(pieces) + [jnp.zeros((head - used, pieces[0].shape[1]), F32)], axis=0)


def chunks(rows):
    return 2 if rows % 32 == 0 else 1


def start_copies(source, target, sems, first=0):
    rows = source.shape[0]
    size = rows // chunks(rows)
    copies = []
    for at in range(chunks(rows)):
        window = pl.ds(at * size, size)
        copies.append(pltpu.make_async_copy(source.at[window], target.at[window], sems.at[first + at]))
        copies[-1].start()
    return copies


def select_block(main, tail, firsts, which, rows, patterns, staged):
    staged[:, 0 : tail.shape[-1]] = tail[pl.ds(firsts[1] + which, rows, stride=patterns), :]
    return jnp.concatenate([main[pl.ds(firsts[0] + which, rows, stride=patterns), :], staged[...]], axis=1)


def pack_kernel(
    bands, count, across, prev, pattern_far, live_far, faces, inverses,
    kept, face_even, face_odd, side_even, side_odd, first, inverse_maps, upstream_maps, masks,
    wide, rows_even, rows_odd, main, tail, inverse_main, inverse_tail, staged, pattern, live, sems,
):
    along = prev.shape[-1]
    rows = prev.shape[0]
    copies = start_copies(prev, kept, sems)
    room, patterns, lanes = main.shape
    ragged = count - lanes
    small = [
        pltpu.make_async_copy(pattern_far, pattern, sems.at[2]),
        pltpu.make_async_copy(live_far, live, sems.at[3]),
    ]
    large = [
        pltpu.make_async_copy(
            inverses.at[:, :, pl.ds(0, lanes)], inverse_main.at[pl.ds(0, count)], sems.at[4]
        ),
        pltpu.make_async_copy(
            inverses.at[:, :, pl.ds(lanes, ragged)], inverse_tail.at[pl.ds(0, count)], sems.at[5]
        ),
        pltpu.make_async_copy(faces.at[0, :, :, pl.ds(0, lanes)], main.at[pl.ds(0, count)], sems.at[6]),
        pltpu.make_async_copy(faces.at[0, :, :, pl.ds(lanes, ragged)], tail.at[pl.ds(0, count)], sems.at[7]),
    ]
    for copy in small + large:
        copy.start()
    staged[...] = jnp.zeros(staged.shape, F32)
    wide[rows:, :] = jnp.zeros((wide.shape[0] - rows, along), F32)
    odd_x = lax.axis_index("cx") % 2 == 1
    odd_y = lax.axis_index("cy") % 2 == 1
    row = lax.broadcasted_iota(jnp.int32, (8, along), 0)
    lane = lax.broadcasted_iota(jnp.int32, (8, along), 1)
    last = along - 1
    even_lane, odd_lane = jnp.where(odd_y, 0, last), jnp.where(odd_y, last, 0)
    chosen = jnp.where(row == 0, even_lane, odd_lane)
    pick = jnp.where(lane == chosen, 1.0, 0.0).astype(BF16)
    size = rows // len(copies)
    done = 0
    for z in range(bands):
        while done * size < min(rows, ((z + 1) * count + 8) * across):
            copies[done].wait()
            window = pl.ds(done * size, size)
            wide[window, :] = kept[window, :].astype(F32)
            done += 1
        blocks = lane_blocks(wide, z * count * across, rest_rows(count), across)
        low, high = blocks[0], blocks[-1]
        face_even[z] = jnp.where(odd_x, low, high).astype(BF16)
        face_odd[z] = jnp.where(odd_x, high, low).astype(BF16)
        for i in range(across):
            found = lax.dot_general(
                pick, blocks[i][0:count].astype(BF16), (((1,), (1,)), ((), ())), preferred_element_type=F32
            )
            at = z * across + i
            rows_even[at : at + 1, :] = found[0:1]
            rows_odd[at : at + 1, :] = found[1:2]
    first[...] = kept[0 : count * across, :]
    side_even[...] = rows_even[...].astype(BF16)
    side_odd[...] = rows_odd[...].astype(BF16)
    for copy in small:
        copy.wait()
    slot = lax.broadcasted_iota(jnp.int32, (1, masks.shape[-1]), 1)
    counts = [live[z] for z in range(bands)]
    before, after = counts[0], counts[bands - 1]
    for z in range(bands):
        before = jnp.minimum(before, counts[z])
        after = jnp.minimum(after, counts[bands - 1 - z])
        for row, limit in ((z, counts[z]), (2 * bands - 1 - z, after), (2 * bands + z, before)):
            masks[row : row + 1, :] = jnp.where(slot < limit, 1.0, 0.0)
    for copy in large:
        copy.wait()
    high_rows = padded_rows(count)
    views = [
        (inverse_main.reshape(room * patterns, lanes), inverse_tail.reshape(room * patterns, ragged), inverse_maps),
        (main.reshape(room * patterns, lanes), tail.reshape(room * patterns, ragged), upstream_maps),
    ]
    for at, (near, rest, target) in enumerate(views):
        for z in range(bands):
            value = select_block(near, rest, (0, 0), pattern[z], high_rows, patterns, staged.at[at * bands + z])
            store_halves(target.at[z], value)


def parts(ref, count):
    start = ref.shape[0] // 2
    return ref[0:count, :], ref[start : start + count, :]


def combine(out, left, right, count):
    store_halves(out, apply_halves(left[...], parts(right, count), out.shape[0] // 2))


def matrix_kernel(
    bands, count, pattern_far, faces, right, inverse_maps, upstream_maps,
    right_kept, maps, step_maps, reach, chains,
    main, tail, pool, staged, pattern, sems,
):
    patterns, lanes = main.shape[1:]
    ragged = count - lanes
    high_rows = padded_rows(count)
    room = tail.shape[1]
    used = tail.shape[0]
    copies = [pltpu.make_async_copy(pattern_far, pattern, sems.at[0])]
    for at in range(used):
        source = faces.at[at + 1]
        copies.append(
            pltpu.make_async_copy(
                source.at[:, :, pl.ds(0, lanes)], main.at[pl.ds(at * count, count)], sems.at[1 + 2 * at]
            )
        )
        copies.append(
            pltpu.make_async_copy(
                source.at[:, :, pl.ds(lanes, ragged)], tail.at[at, pl.ds(0, count)], sems.at[2 + 2 * at]
            )
        )
    copies.append(pltpu.make_async_copy(right, right_kept, sems.at[1 + 2 * used]))
    for copy in copies:
        copy.start()
    staged[...] = jnp.zeros(staged.shape, F32)
    main_rows = main.reshape(main.shape[0] * patterns, lanes)
    tail_rows = tail.reshape(used * room * patterns, ragged)

    def selected(band, face):
        at = face - 1
        firsts = (at * count * patterns, at * room * patterns)
        return select_block(
            main_rows, tail_rows, firsts, pattern[band], high_rows, patterns, staged.at[at * bands + band]
        )

    for z in range(bands):
        upstream = parts(upstream_maps.at[z], count)
        store_halves(step_maps.at[z], -apply_halves(inverse_maps[z], upstream, high_rows))
    spare = [0]

    def fresh():
        spare[0] += 1
        return pool.at[spare[0] - 1]

    def solve(low, high, top):
        if high - low == 1:
            return {low: inverse_maps.at[low]}, step_maps.at[low]
        middle = (low + high) // 2
        near, near_step = solve(low, middle, False)
        found, far_step = solve(middle, high, False)
        for z, ref in near.items():
            found[z] = fresh()
            combine(found[z], far_step, ref, count)
        step = None
        if not top:
            step = fresh()
            combine(step, far_step, near_step, count)
        return found, step

    full_reach, _ = solve(0, bands, True)
    chains[0] = step_maps[0]
    for z in range(1, bands):
        combine(chains.at[z], step_maps.at[z], chains.at[z - 1], count)

    def put(ref, tile, value):
        high, low = halves(value)
        window = pl.ds(tile * lanes, lanes)
        ref[0:high_rows, window] = high
        ref[high_rows : 2 * high_rows, window] = low

    rests = [None] * bands
    total = maps.shape[2] // lanes - 1

    for copy in copies:
        copy.wait()

    def take(face):
        for z in range(bands):
            value = selected(z, face)
            put(maps.at[z], face - 1, value[:, :lanes])
            rest = pltpu.roll(value[:, lanes:], 8 * (face - 1), axis=1)
            rests[z] = rest if rests[z] is None else rests[z] + rest

    for face in range(1, used + 1):
        take(face)
    reach_rest = None
    for z in range(bands):
        put(maps.at[z], total, rests[z])
        natural = full_reach[z]
        reach[:, pl.ds(z * lanes, lanes)] = natural[:, 0:lanes]
        rest = natural[0:high_rows, lanes:].astype(F32) + natural[high_rows:, lanes:].astype(F32)
        rest = pltpu.roll(rest, 8 * z, axis=1)
        reach_rest = rest if reach_rest is None else reach_rest + rest
    put(reach, bands, reach_rest)


def local_kernel(
    bands, count, across, right, prev, follow, side_even, side_odd, face_even, face_odd, maps, reach, masks,
    base, last_band, wide, wide_right, wide_follow, sides, stacks, high_stack, low_stack,
):
    along = prev.shape[-1]
    rows = prev.shape[0]
    block = count * across
    deep = rest_rows(count)
    head = count // 128 * 128
    odd_y = lax.axis_index("cy") % 2 == 1
    has_next = lax.axis_index("sweep") < lax.axis_size("sweep") - 1
    wide[0:rows, :] = prev[...].astype(F32)
    wide_right[0:rows, :] = right[...].astype(F32)
    wide_follow[0:block, :] = jnp.where(has_next, follow[...].astype(F32), 0.0)
    even, odd = side_even[...].astype(F32), side_odd[...].astype(F32)
    total = bands * across
    sides[0:total, 0:count] = jnp.where(odd_y, even, odd)
    sides[total : 2 * total, 0:count] = jnp.where(odd_y, odd, even)
    columns = sides[...].T
    lane = lax.broadcasted_iota(jnp.int32, (deep, along), 1)
    heads, rests = [], []
    for z in range(bands + 1):
        blocks = lane_blocks(*((wide, z * block) if z < bands else (wide_follow, 0)), deep, across)
        heads.append([value[0:head].astype(BF16) for value in blocks])
        rests.append([rest_of(value, head, count) for value in blocks])
        if z == bands:
            continue
        for i, value in enumerate(blocks):
            window = pl.ds(i * along, along)
            at = z * across + i
            column = columns[0:deep, at : at + 1]
            behind = jnp.where(lane == 0, column, pltpu.roll(value, 1, axis=1))
            column = columns[0:deep, at + total : at + total + 1]
            ahead = jnp.where(lane == along - 1, column, pltpu.roll(value, along - 1, axis=1))
            stacks[z, 3 * head : 4 * head, window] = behind[0:head].astype(BF16)
            stacks[z, 4 * head : 5 * head, window] = ahead[0:head].astype(BF16)
            rests[z][i] = (rests[z][i], rest_of(behind, head, count), rest_of(ahead, head, count))
    final_rests = []
    for z in range(bands):
        minus, plus = edges_of(face_even, face_odd, z)
        for i in range(across):
            window = pl.ds(i * along, along)
            first, last = i == 0, i == across - 1
            stacks[z, 0:head, window] = heads[z + 1][i]
            stacks[z, head : 2 * head, window] = minus[0:head].astype(BF16) if first else heads[z][i - 1]
            stacks[z, 2 * head : 3 * head, window] = plus[0:head].astype(BF16) if last else heads[z][i + 1]
            _, behind, ahead = rests[z][i]
            pieces = [
                rests[z + 1][i][0] if z + 1 < bands else rests[z + 1][i],
                rest_of(minus, head, count) if first else rests[z][i - 1][0],
                rest_of(plus, head, count) if last else rests[z][i + 1][0],
                behind,
                ahead,
            ]
            stacks[z, 5 * head : 6 * head, window] = stacked_rests(pieces, head).astype(BF16)
        drop = apply(maps[z], stacks[z], deep)
        value = jnp.concatenate(lane_blocks(wide_right, z * block, deep, across), axis=1) - drop
        base[z] = value[0:count]
        value = value * masks[bands + z : bands + z + 1, :]
        high, low = halves(value[0:head])
        high_stack[z * head : (z + 1) * head, :] = high
        low_stack[z * head : (z + 1) * head, :] = low
        final_rests.append(rest_of(value, head, count))
    high, low = halves(stacked_rests(final_rests, head))
    high_stack[bands * head :, :] = high
    low_stack[bands * head :, :] = low
    last_band[...] = apply_halves(reach[...], (high_stack[...], low_stack[...]), count)


def edges_of(face_even, face_odd, z):
    odd_x = lax.axis_index("cx") % 2 == 1
    even, odd = face_even[z].astype(F32), face_odd[z].astype(F32)
    return jnp.where(odd_x, even, odd), jnp.where(odd_x, odd, even)


def sweep_kernel(bands, count, base, masks, inverse_maps, step_maps, states):
    shares = [apply_halves(inverse_maps[z], halves(base[z]), count) for z in range(bands)]
    current = None
    for z in range(bands):
        value = shares[z]
        if z > 0:
            value = value + apply_halves(step_maps[z], halves(current), count)
        current = value * masks[z : z + 1, :]
        states[z] = current


def finish_kernel(bands, count, across, masks, states, chains, incoming, out, staged, sems):
    cells = incoming.shape[-1]
    along = cells // across
    rows = staged.shape[0]
    right = halves(jnp.where(lax.axis_index("sweep") > 0, incoming[...], 0.0))
    size = rows // chunks(rows)
    copies = []
    for z in range(bands):
        moved = apply_halves(chains[z], right, count)
        value = states[z] + moved * masks[2 * bands + z : 2 * bands + z + 1, :]
        for i in range(across):
            staged[pl.ds(z * count * across + i, count, stride=across), :] = value[:, i * along : (i + 1) * along]
        while (len(copies) + 1) * size <= (z + 1) * count * across:
            at = len(copies)
            window = pl.ds(at * size, size)
            copies.append(pltpu.make_async_copy(staged.at[window], out.at[window], sems.at[at]))
            copies[-1].start()
    for copy in copies:
        copy.wait()


def call(kernel, out, specs, scratch=(), flops=0, moved=0, out_specs=None):
    return pl.pallas_call(
        kernel,
        out_shape=out,
        in_specs=specs,
        out_specs=out_specs or jax.tree.map(lambda _: VMEM, out),
        scratch_shapes=scratch,
        cost_estimate=pl.CostEstimate(flops=flops, bytes_accessed=moved, transcendentals=0),
        compiler_params=pltpu.CompilerParams(vmem_limit_bytes=32 * 2**20),
    )


def in_hbm(value):
    return pltpu.with_memory_space_constraint(value, pltpu.HBM)


def swapped(value, axis, first):
    pairs = []
    for left in range(first, lax.axis_size(axis) - 1, 2):
        pairs += [(left, left + 1), (left + 1, left)]
    return lax.ppermute(value, axis, pairs)


def passed_along(value, axis, steps):
    count = lax.axis_size(axis)
    if count == 2:
        return swapped(value, axis, 0)
    first, last = (max(0, -steps), min(count, count - steps))
    return lax.ppermute(value, axis, [(source, source + steps) for source in range(first, last)])


def on_device(right_side, previous, diag_inverse, face_blocks, pattern, live_count):
    bands, count, across, along = right_side.shape
    cells, rows = across * along, bands * count * across
    pads, wide_count = 2 * padded_rows(count), rounded(count, 128)
    shape = jax.ShapeDtypeStruct
    patterns, face_total = face_blocks.shape[:2]
    lanes = count // 128 * 128
    right = in_hbm(right_side.reshape(rows, along))
    prev = in_hbm(previous.reshape(rows, along))
    faces = in_hbm(face_blocks.transpose(1, 2, 0, 3))
    inverses = in_hbm(diag_inverse.transpose(1, 0, 2))
    live = in_hbm(live_count.reshape(bands))
    pattern = in_hbm(pattern)
    deep = rest_rows(count)
    face = shape((bands, deep, along), BF16)
    side = shape((bands * across, count), BF16)
    field = shape((rows, along), BF16)
    side_rows = pltpu.VMEM((bands * across, count), F32)
    filled = pltpu.VMEM((rows + 8 * across, along), F32)
    wide = pltpu.VMEM((rows, along), F32)
    matrix = shape((bands, pads, wide_count), BF16)
    block_room = [
        pltpu.VMEM((count + 16, patterns, lanes), F32),
        pltpu.VMEM((count + 16, patterns, count - lanes), F32),
    ]
    small_room = pltpu.SMEM((bands,), jnp.int32)
    (
        kept, face_even, face_odd, side_even, side_odd, first, inverse_maps, upstream_maps, masks
    ) = call(
        functools.partial(pack_kernel, bands, count, across),
        (
            field,
            face,
            face,
            side,
            side,
            shape((count * across, along), BF16),
            matrix,
            matrix,
            shape((3 * bands, cells), F32),
        ),
        [HBM] * 5,
        [filled, side_rows, side_rows]
        + block_room * 2
        + [pltpu.VMEM((2 * bands, pads // 2, lanes), F32), small_room, small_room, pltpu.SemaphoreType.DMA((8,))],
        moved=rows * along * 4,
    )(prev, pattern, live, faces, inverses)
    side_even = swapped(side_even, "cy", 0)
    side_odd = swapped(side_odd, "cy", 1)
    follow = passed_along(first, "sweep", -1)
    face_odd = swapped(face_odd, "cx", 1)
    face_even = swapped(face_even, "cx", 0)
    step_flops = count * count * cells * 2
    used = face_total - 1
    right_kept, maps, step_maps, reach, chains = call(
        functools.partial(matrix_kernel, bands, count),
        (
            field,
            shape((bands, pads, face_total * lanes), BF16),
            matrix,
            shape((pads, (bands + 1) * lanes), BF16),
            matrix,
        ),
        [HBM, HBM, HBM, VMEM, VMEM],
        [
            pltpu.VMEM((used * count + 16, patterns, lanes), F32),
            pltpu.VMEM((used, count + 16, patterns, count - lanes), F32),
            pltpu.VMEM((4 * bands, pads, wide_count), BF16),
            pltpu.VMEM((used * bands, pads // 2, lanes), F32),
            small_room,
            pltpu.SemaphoreType.DMA((2 * used + 2,)),
        ],
        flops=bands * 5 * step_flops,
        moved=4 * 2**20,
    )(pattern, faces, right, inverse_maps, upstream_maps)
    base, last = call(
        functools.partial(local_kernel, bands, count, across),
        (shape((bands, count, cells), F32), shape((count, cells), F32)),
        [VMEM] * 10,
        [
            filled,
            filled,
            pltpu.VMEM(((count + 8) * across, along), F32),
            pltpu.VMEM((rounded(2 * bands * across, 128), rounded(count, 128)), F32),
            pltpu.VMEM((bands, face_total * lanes, cells), BF16),
            pltpu.VMEM(((bands + 1) * lanes, cells), BF16),
            pltpu.VMEM(((bands + 1) * lanes, cells), BF16),
        ],
        flops=bands * 13 * step_flops,
        moved=2**20,
    )(right_kept, kept, follow, side_even, side_odd, face_even, face_odd, maps, reach, masks)
    states = call(
        functools.partial(sweep_kernel, bands, count),
        shape((bands, count, cells), F32),
        [VMEM] * 4,
        flops=bands * 7 * step_flops,
        moved=2**20,
    )(base, masks, inverse_maps, step_maps)
    incoming = passed_along(last, "sweep", 1)
    if lax.axis_size("sweep") > 2:
        start = padded_rows(count)
        end_map = chains[-1, 0:count, 0:count].astype(F32) + chains[-1, start : start + count, 0:count].astype(F32)
        slot = jnp.arange(cells, dtype=jnp.int32)
        kept = (slot < jnp.min(live_count)).astype(F32)

        def relay(_, arriving):
            product = jnp.dot(end_map, arriving, precision=lax.Precision.HIGHEST)
            return passed_along(last + kept[None, :] * product, "sweep", 1)

        incoming = lax.fori_loop(0, lax.axis_size("sweep") - 2, relay, incoming)
    out = call(
        functools.partial(finish_kernel, bands, count, across),
        shape((rows, along), F32),
        [VMEM] * 4,
        [wide, pltpu.SemaphoreType.DMA((2,))],
        flops=bands * 3 * step_flops,
        moved=2**20,
        out_specs=HBM,
    )(masks, states, chains, incoming)
    return out.reshape(bands, count, across, along)


def solution(mesh):
    return jax.shard_map(
        on_device,
        mesh=mesh,
        in_specs=(
            P("sweep", None, "cx", "cy"),
            P("sweep", None, "cx", "cy"),
            P(),
            P(),
            P("sweep"),
            P("sweep", "cx", "cy"),
        ),
        out_specs=P("sweep", None, "cx", "cy"),
        check_vma=False,
    )
```

```python
import functools

import jax
import jax.numpy as jnp
from jax import lax
from jax.experimental import pallas as pl
from jax.experimental.pallas import tpu as pltpu
from jax.sharding import PartitionSpec as P


F32, BF16 = jnp.float32, jnp.bfloat16
VMEM = pl.BlockSpec(memory_space=pltpu.VMEM)
HBM = pl.BlockSpec(memory_space=pltpu.HBM)


def rounded(count, unit):
    return (count + unit - 1) // unit * unit


def padded_rows(count):
    return rounded(count, 16)


def product(left, right):
    return jnp.dot(left, right, preferred_element_type=F32)


def halves(value):
    high = value.astype(BF16)
    return high, (value - high.astype(F32)).astype(BF16)


def store_halves(ref, value):
    high, low = halves(value)
    start = value.shape[0]
    ref[0:start, :] = high
    ref[start : 2 * start, :] = low


def apply(stacked, right, rows):
    both = product(stacked[:, : right.shape[0]], right)
    start = stacked.shape[0] // 2
    return both[0:rows] + both[start : start + rows]


def apply_halves(stacked, right, rows):
    high, low = right
    start = stacked.shape[0] // 2
    rest = product(stacked[0:start, : low.shape[0]], low)
    return apply(stacked, high, rows) + rest[0:rows]


def lane_blocks(ref, start, count, across):
    return [ref[pl.ds(start + i, count, stride=across), :] for i in range(across)]


def rest_rows(count):
    return rounded(count, 8)


def rest_of(value, head, count):
    piece = value[head:]
    row = lax.broadcasted_iota(jnp.int32, piece.shape, 0)
    return jnp.where(row < count - head, piece, 0.0)


def stacked_rests(pieces, head):
    used = sum(piece.shape[0] for piece in pieces)
    return jnp.concatenate(list(pieces) + [jnp.zeros((head - used, pieces[0].shape[1]), F32)], axis=0)


def chunks(rows):
    return 2 if rows % 32 == 0 else 1


def start_copies(source, target, sems, first=0):
    rows = source.shape[0]
    size = rows // chunks(rows)
    copies = []
    for at in range(chunks(rows)):
        window = pl.ds(at * size, size)
        copies.append(pltpu.make_async_copy(source.at[window], target.at[window], sems.at[first + at]))
        copies[-1].start()
    return copies


def select_block(main, tail, firsts, which, rows, patterns, staged):
    staged[:, 0 : tail.shape[-1]] = tail[pl.ds(firsts[1] + which, rows, stride=patterns), :]
    return jnp.concatenate([main[pl.ds(firsts[0] + which, rows, stride=patterns), :], staged[...]], axis=1)


def pack_kernel(
    bands, count, across, prev, pattern_far, live_far, faces, inverses,
    kept, face_even, face_odd, side_even, side_odd, first, inverse_maps, upstream_maps, masks,
    wide, rows_even, rows_odd, main, tail, inverse_main, inverse_tail, staged, pattern, live, sems,
):
    along = prev.shape[-1]
    rows = prev.shape[0]
    copies = start_copies(prev, kept, sems)
    room, patterns, lanes = main.shape
    ragged = count - lanes
    small = [
        pltpu.make_async_copy(pattern_far, pattern, sems.at[2]),
        pltpu.make_async_copy(live_far, live, sems.at[3]),
    ]
    large = [
        pltpu.make_async_copy(
            inverses.at[:, :, pl.ds(0, lanes)], inverse_main.at[pl.ds(0, count)], sems.at[4]
        ),
        pltpu.make_async_copy(
            inverses.at[:, :, pl.ds(lanes, ragged)], inverse_tail.at[pl.ds(0, count)], sems.at[5]
        ),
        pltpu.make_async_copy(faces.at[0, :, :, pl.ds(0, lanes)], main.at[pl.ds(0, count)], sems.at[6]),
        pltpu.make_async_copy(faces.at[0, :, :, pl.ds(lanes, ragged)], tail.at[pl.ds(0, count)], sems.at[7]),
    ]
    for copy in small + large:
        copy.start()
    staged[...] = jnp.zeros(staged.shape, F32)
    wide[rows:, :] = jnp.zeros((wide.shape[0] - rows, along), F32)
    odd_x = lax.axis_index("cx") % 2 == 1
    odd_y = lax.axis_index("cy") % 2 == 1
    row = lax.broadcasted_iota(jnp.int32, (8, along), 0)
    lane = lax.broadcasted_iota(jnp.int32, (8, along), 1)
    last = along - 1
    even_lane, odd_lane = jnp.where(odd_y, 0, last), jnp.where(odd_y, last, 0)
    chosen = jnp.where(row == 0, even_lane, odd_lane)
    pick = jnp.where(lane == chosen, 1.0, 0.0).astype(BF16)
    size = rows // len(copies)
    done = 0
    for z in range(bands):
        while done * size < min(rows, ((z + 1) * count + 8) * across):
            copies[done].wait()
            window = pl.ds(done * size, size)
            wide[window, :] = kept[window, :].astype(F32)
            done += 1
        blocks = lane_blocks(wide, z * count * across, rest_rows(count), across)
        low, high = blocks[0], blocks[-1]
        face_even[z] = jnp.where(odd_x, low, high).astype(BF16)
        face_odd[z] = jnp.where(odd_x, high, low).astype(BF16)
        for i in range(across):
            found = lax.dot_general(
                pick, blocks[i][0:count].astype(BF16), (((1,), (1,)), ((), ())), preferred_element_type=F32
            )
            at = z * across + i
            rows_even[at : at + 1, :] = found[0:1]
            rows_odd[at : at + 1, :] = found[1:2]
    first[...] = kept[0 : count * across, :]
    side_even[...] = rows_even[...].astype(BF16)
    side_odd[...] = rows_odd[...].astype(BF16)
    for copy in small:
        copy.wait()
    slot = lax.broadcasted_iota(jnp.int32, (1, masks.shape[-1]), 1)
    counts = [live[z] for z in range(bands)]
    before, after = counts[0], counts[bands - 1]
    for z in range(bands):
        before = jnp.minimum(before, counts[z])
        after = jnp.minimum(after, counts[bands - 1 - z])
        for row, limit in ((z, counts[z]), (2 * bands - 1 - z, after), (2 * bands + z, before)):
            masks[row : row + 1, :] = jnp.where(slot < limit, 1.0, 0.0)
    for copy in large:
        copy.wait()
    high_rows = padded_rows(count)
    views = [
        (inverse_main.reshape(room * patterns, lanes), inverse_tail.reshape(room * patterns, ragged), inverse_maps),
        (main.reshape(room * patterns, lanes), tail.reshape(room * patterns, ragged), upstream_maps),
    ]
    for at, (near, rest, target) in enumerate(views):
        for z in range(bands):
            value = select_block(near, rest, (0, 0), pattern[z], high_rows, patterns, staged.at[at * bands + z])
            store_halves(target.at[z], value)


def parts(ref, count):
    start = ref.shape[0] // 2
    return ref[0:count, :], ref[start : start + count, :]


def combine(out, left, right, count):
    store_halves(out, apply_halves(left[...], parts(right, count), out.shape[0] // 2))


def matrix_kernel(
    bands, count, pattern_far, faces, right, inverse_maps, upstream_maps,
    right_kept, maps, step_maps, reach, chains,
    main, tail, pool, staged, pattern, sems,
):
    patterns, lanes = main.shape[1:]
    ragged = count - lanes
    high_rows = padded_rows(count)
    room = tail.shape[1]
    used = tail.shape[0]
    copies = [pltpu.make_async_copy(pattern_far, pattern, sems.at[0])]
    for at in range(used):
        source = faces.at[at + 1]
        copies.append(
            pltpu.make_async_copy(
                source.at[:, :, pl.ds(0, lanes)], main.at[pl.ds(at * count, count)], sems.at[1 + 2 * at]
            )
        )
        copies.append(
            pltpu.make_async_copy(
                source.at[:, :, pl.ds(lanes, ragged)], tail.at[at, pl.ds(0, count)], sems.at[2 + 2 * at]
            )
        )
    copies.append(pltpu.make_async_copy(right, right_kept, sems.at[1 + 2 * used]))
    for copy in copies:
        copy.start()
    staged[...] = jnp.zeros(staged.shape, F32)
    main_rows = main.reshape(main.shape[0] * patterns, lanes)
    tail_rows = tail.reshape(used * room * patterns, ragged)

    def selected(band, face):
        at = face - 1
        firsts = (at * count * patterns, at * room * patterns)
        return select_block(
            main_rows, tail_rows, firsts, pattern[band], high_rows, patterns, staged.at[at * bands + band]
        )

    for z in range(bands):
        upstream = parts(upstream_maps.at[z], count)
        store_halves(step_maps.at[z], -apply_halves(inverse_maps[z], upstream, high_rows))
    spare = [0]

    def fresh():
        spare[0] += 1
        return pool.at[spare[0] - 1]

    def solve(low, high, top):
        if high - low == 1:
            return {low: inverse_maps.at[low]}, step_maps.at[low]
        middle = (low + high) // 2
        near, near_step = solve(low, middle, False)
        found, far_step = solve(middle, high, False)
        for z, ref in near.items():
            found[z] = fresh()
            combine(found[z], far_step, ref, count)
        step = None
        if not top:
            step = fresh()
            combine(step, far_step, near_step, count)
        return found, step

    full_reach, _ = solve(0, bands, True)
    chains[0] = step_maps[0]
    for z in range(1, bands):
        combine(chains.at[z], step_maps.at[z], chains.at[z - 1], count)

    def put(ref, tile, value):
        high, low = halves(value)
        window = pl.ds(tile * lanes, lanes)
        ref[0:high_rows, window] = high
        ref[high_rows : 2 * high_rows, window] = low

    rests = [None] * bands
    total = maps.shape[2] // lanes - 1

    copies[0].wait()

    def take(face):
        for copy in copies[2 * face - 1 : 2 * face + 1]:
            copy.wait()
        for z in range(bands):
            value = selected(z, face)
            put(maps.at[z], face - 1, value[:, :lanes])
            rest = pltpu.roll(value[:, lanes:], 8 * (face - 1), axis=1)
            rests[z] = rest if rests[z] is None else rests[z] + rest

    reach_rest = None
    for z in range(bands):
        natural = full_reach[z]
        reach[:, pl.ds(z * lanes, lanes)] = natural[:, 0:lanes]
        rest = natural[0:high_rows, lanes:].astype(F32) + natural[high_rows:, lanes:].astype(F32)
        rest = pltpu.roll(rest, 8 * z, axis=1)
        reach_rest = rest if reach_rest is None else reach_rest + rest
    put(reach, bands, reach_rest)
    for face in range(1, used + 1):
        take(face)
    for z in range(bands):
        put(maps.at[z], total, rests[z])
    copies[-1].wait()


def local_kernel(
    bands, count, across, right, prev, follow, side_even, side_odd, face_even, face_odd, maps, reach, masks,
    base, last_band, heads, rests, wide, wide_right, wide_follow, sides, shifted, rest_stacks, high_stack, low_stack,
):
    rows, along = right.shape
    block = count * across
    deep = rest_rows(count)
    head = count // 128 * 128
    edge = (across - 1) * along
    odd_y = lax.axis_index("cy") % 2 == 1
    has_next = lax.axis_index("sweep") < lax.axis_size("sweep") - 1
    wide[0:rows, :] = prev[...].astype(F32)
    for z in range(bands):
        for i, value in enumerate(lane_blocks(wide, z * block, deep, across)):
            window = pl.ds(i * along, along)
            heads[z, :, window] = value[0:head].astype(BF16)
            rests[z, :, window] = rest_of(value, head, count)
    wide_right[0:rows, :] = right[...].astype(F32)
    wide_follow[0:block, :] = jnp.where(has_next, follow[...].astype(F32), 0.0)
    even, odd = side_even[...].astype(F32), side_odd[...].astype(F32)
    total = bands * across
    sides[0:total, 0:count] = jnp.where(odd_y, even, odd)
    sides[total : 2 * total, 0:count] = jnp.where(odd_y, odd, even)
    columns = sides[...].T
    lane = lax.broadcasted_iota(jnp.int32, (deep, along), 1)
    beyond = lane_blocks(wide_follow, 0, deep, across)
    beyond_head = jnp.concatenate([value[0:head].astype(BF16) for value in beyond], axis=1)
    beyond_rest = jnp.concatenate([rest_of(value, head, count) for value in beyond], axis=1)
    final_rests = []
    for z in range(bands):
        minus, plus = edges_of(face_even, face_odd, z)
        behind_rests, ahead_rests = [], []
        for i in range(across):
            window = slice(i * along, (i + 1) * along)
            value = jnp.concatenate([heads[z, :, window].astype(F32), rests[z, :, window]], axis=0)
            at = z * across + i
            column = columns[0:deep, at : at + 1]
            behind = jnp.where(lane == 0, column, pltpu.roll(value, 1, axis=1))
            column = columns[0:deep, at + total : at + total + 1]
            ahead = jnp.where(lane == along - 1, column, pltpu.roll(value, along - 1, axis=1))
            shifted[z, 0:head, window] = behind[0:head].astype(BF16)
            shifted[z, head:, window] = ahead[0:head].astype(BF16)
            behind_rests.append(rest_of(behind, head, count))
            ahead_rests.append(rest_of(ahead, head, count))
        own, own_rest = heads[z], rests[z]
        pieces = [
            rests[z + 1] if z + 1 < bands else beyond_rest,
            jnp.concatenate([rest_of(minus, head, count), own_rest[:, :edge]], axis=1),
            jnp.concatenate([own_rest[:, along:], rest_of(plus, head, count)], axis=1),
            jnp.concatenate(behind_rests, axis=1),
            jnp.concatenate(ahead_rests, axis=1),
        ]
        rest_stacks[z] = stacked_rests(pieces, head).astype(BF16)
        fields = jnp.concatenate(
            [
                heads[z + 1] if z + 1 < bands else beyond_head,
                jnp.concatenate([minus[0:head].astype(BF16), own[:, :edge]], axis=1),
                jnp.concatenate([own[:, along:], plus[0:head].astype(BF16)], axis=1),
                shifted[z],
                rest_stacks[z],
            ],
            axis=0,
        )
        drop = apply(maps[z], fields, deep)
        value = jnp.concatenate(lane_blocks(wide_right, z * block, deep, across), axis=1) - drop
        base[z] = value[0:count]
        value = value * masks[bands + z : bands + z + 1, :]
        high, low = halves(value[0:head])
        high_stack[z * head : (z + 1) * head, :] = high
        low_stack[z * head : (z + 1) * head, :] = low
        final_rests.append(rest_of(value, head, count))
    high, low = halves(stacked_rests(final_rests, head))
    high_stack[bands * head :, :] = high
    low_stack[bands * head :, :] = low
    last_band[...] = apply_halves(reach[...], (high_stack[...], low_stack[...]), count)


def edges_of(face_even, face_odd, z):
    odd_x = lax.axis_index("cx") % 2 == 1
    even, odd = face_even[z].astype(F32), face_odd[z].astype(F32)
    return jnp.where(odd_x, even, odd), jnp.where(odd_x, odd, even)


def sweep_kernel(bands, count, base, masks, inverse_maps, step_maps, states):
    shares = [apply_halves(inverse_maps[z], halves(base[z]), count) for z in range(bands)]
    current = None
    for z in range(bands):
        value = shares[z]
        if z > 0:
            value = value + apply_halves(step_maps[z], halves(current), count)
        current = value * masks[z : z + 1, :]
        states[z] = current


def finish_kernel(bands, count, across, masks, states, chains, incoming, out, staged, sems):
    cells = incoming.shape[-1]
    along = cells // across
    rows = staged.shape[0]
    right = halves(jnp.where(lax.axis_index("sweep") > 0, incoming[...], 0.0))
    copies = []
    sent = 0
    for z in range(bands):
        moved = apply_halves(chains[z], right, count)
        value = states[z] + moved * masks[2 * bands + z : 2 * bands + z + 1, :]
        for i in range(across):
            staged[pl.ds(z * count * across + i, count, stride=across), :] = value[:, i * along : (i + 1) * along]
        ready = (z + 1) * count * across
        ready = rows if ready == rows else ready // 8 * 8
        window = pl.ds(sent, ready - sent)
        copies.append(pltpu.make_async_copy(staged.at[window], out.at[window], sems.at[z]))
        copies[-1].start()
        sent = ready
    for copy in copies:
        copy.wait()


def call(kernel, out, specs, scratch=(), flops=0, moved=0, out_specs=None):
    return pl.pallas_call(
        kernel,
        out_shape=out,
        in_specs=specs,
        out_specs=out_specs or jax.tree.map(lambda _: VMEM, out),
        scratch_shapes=scratch,
        cost_estimate=pl.CostEstimate(flops=flops, bytes_accessed=moved, transcendentals=0),
        compiler_params=pltpu.CompilerParams(vmem_limit_bytes=32 * 2**20),
    )


def in_hbm(value):
    return pltpu.with_memory_space_constraint(value, pltpu.HBM)


def swapped(value, axis, first):
    pairs = []
    for left in range(first, lax.axis_size(axis) - 1, 2):
        pairs += [(left, left + 1), (left + 1, left)]
    return lax.ppermute(value, axis, pairs)


def passed_along(value, axis, steps):
    count = lax.axis_size(axis)
    if count == 2:
        return swapped(value, axis, 0)
    first, last = (max(0, -steps), min(count, count - steps))
    return lax.ppermute(value, axis, [(source, source + steps) for source in range(first, last)])


def on_device(right_side, previous, diag_inverse, face_blocks, pattern, live_count):
    bands, count, across, along = right_side.shape
    cells, rows = across * along, bands * count * across
    pads, wide_count = 2 * padded_rows(count), rounded(count, 128)
    shape = jax.ShapeDtypeStruct
    patterns, face_total = face_blocks.shape[:2]
    lanes = count // 128 * 128
    right = in_hbm(right_side.reshape(rows, along))
    prev = in_hbm(previous.reshape(rows, along))
    faces = in_hbm(face_blocks.transpose(1, 2, 0, 3))
    inverses = in_hbm(diag_inverse.transpose(1, 0, 2))
    live = in_hbm(live_count.reshape(bands))
    pattern = in_hbm(pattern)
    deep = rest_rows(count)
    face = shape((bands, deep, along), BF16)
    side = shape((bands * across, count), BF16)
    field = shape((rows, along), BF16)
    side_rows = pltpu.VMEM((bands * across, count), F32)
    filled = pltpu.VMEM((rows + 8 * across, along), F32)
    wide = pltpu.VMEM((rows, along), F32)
    matrix = shape((bands, pads, wide_count), BF16)
    block_room = [
        pltpu.VMEM((count + 16, patterns, lanes), F32),
        pltpu.VMEM((count + 16, patterns, count - lanes), F32),
    ]
    small_room = pltpu.SMEM((bands,), jnp.int32)
    (
        kept, face_even, face_odd, side_even, side_odd, first, inverse_maps, upstream_maps, masks
    ) = call(
        functools.partial(pack_kernel, bands, count, across),
        (
            field,
            face,
            face,
            side,
            side,
            shape((count * across, along), BF16),
            matrix,
            matrix,
            shape((3 * bands, cells), F32),
        ),
        [HBM] * 5,
        [filled, side_rows, side_rows]
        + block_room * 2
        + [pltpu.VMEM((2 * bands, pads // 2, lanes), F32), small_room, small_room, pltpu.SemaphoreType.DMA((8,))],
        moved=rows * along * 4,
    )(prev, pattern, live, faces, inverses)
    side_even = swapped(side_even, "cy", 0)
    side_odd = swapped(side_odd, "cy", 1)
    follow = passed_along(first, "sweep", -1)
    face_odd = swapped(face_odd, "cx", 1)
    face_even = swapped(face_even, "cx", 0)
    step_flops = count * count * cells * 2
    used = face_total - 1
    right_kept, maps, step_maps, reach, chains = call(
        functools.partial(matrix_kernel, bands, count),
        (
            field,
            shape((bands, pads, face_total * lanes), BF16),
            matrix,
            shape((pads, (bands + 1) * lanes), BF16),
            matrix,
        ),
        [HBM, HBM, HBM, VMEM, VMEM],
        [
            pltpu.VMEM((used * count + 16, patterns, lanes), F32),
            pltpu.VMEM((used, count + 16, patterns, count - lanes), F32),
            pltpu.VMEM((4 * bands, pads, wide_count), BF16),
            pltpu.VMEM((used * bands, pads // 2, lanes), F32),
            small_room,
            pltpu.SemaphoreType.DMA((2 * used + 2,)),
        ],
        flops=bands * 5 * step_flops,
        moved=4 * 2**20,
    )(pattern, faces, right, inverse_maps, upstream_maps)
    base, last = call(
        functools.partial(local_kernel, bands, count, across),
        (shape((bands, count, cells), F32), shape((count, cells), F32)),
        [VMEM] * 10,
        [
            pltpu.VMEM((bands, lanes, cells), BF16),
            pltpu.VMEM((bands, deep - lanes, cells), F32),
            filled,
            filled,
            pltpu.VMEM(((count + 8) * across, along), F32),
            pltpu.VMEM((rounded(2 * bands * across, 128), rounded(count, 128)), F32),
            pltpu.VMEM((bands, 2 * lanes, cells), BF16),
            pltpu.VMEM((bands, lanes, cells), BF16),
            pltpu.VMEM(((bands + 1) * lanes, cells), BF16),
            pltpu.VMEM(((bands + 1) * lanes, cells), BF16),
        ],
        flops=bands * 13 * step_flops,
        moved=2**20,
    )(right_kept, kept, follow, side_even, side_odd, face_even, face_odd, maps, reach, masks)
    states = call(
        functools.partial(sweep_kernel, bands, count),
        shape((bands, count, cells), F32),
        [VMEM] * 4,
        flops=bands * 7 * step_flops,
        moved=2**20,
    )(base, masks, inverse_maps, step_maps)
    incoming = passed_along(last, "sweep", 1)
    if lax.axis_size("sweep") > 2:
        start = padded_rows(count)
        end_map = chains[-1, 0:count, 0:count].astype(F32) + chains[-1, start : start + count, 0:count].astype(F32)
        slot = jnp.arange(cells, dtype=jnp.int32)
        kept = (slot < jnp.min(live_count)).astype(F32)

        def relay(_, arriving):
            product = jnp.dot(end_map, arriving, precision=lax.Precision.HIGHEST)
            return passed_along(last + kept[None, :] * product, "sweep", 1)

        incoming = lax.fori_loop(0, lax.axis_size("sweep") - 2, relay, incoming)
    out = call(
        functools.partial(finish_kernel, bands, count, across),
        shape((rows, along), F32),
        [VMEM] * 4,
        [wide, pltpu.SemaphoreType.DMA((bands,))],
        flops=bands * 3 * step_flops,
        moved=2**20,
        out_specs=HBM,
    )(masks, states, chains, incoming)
    return out.reshape(bands, count, across, along)


def solution(mesh):
    return jax.shard_map(
        on_device,
        mesh=mesh,
        in_specs=(
            P("sweep", None, "cx", "cy"),
            P("sweep", None, "cx", "cy"),
            P(),
            P(),
            P("sweep"),
            P("sweep", "cx", "cy"),
        ),
        out_specs=P("sweep", None, "cx", "cy"),
        check_vma=False,
    )
```

```python
import functools

import jax
import jax.numpy as jnp
from jax import lax
from jax.experimental import pallas as pl
from jax.experimental.pallas import tpu as pltpu
from jax.sharding import PartitionSpec as P


F32, BF16 = jnp.float32, jnp.bfloat16
VMEM = pl.BlockSpec(memory_space=pltpu.VMEM)
HBM = pl.BlockSpec(memory_space=pltpu.HBM)


def rounded(count, unit):
    return (count + unit - 1) // unit * unit


def padded_rows(count):
    return rounded(count, 16)


def product(left, right):
    return jnp.dot(left, right, preferred_element_type=F32)


def halves(value):
    high = value.astype(BF16)
    return high, (value - high.astype(F32)).astype(BF16)


def store_halves(ref, value):
    high, low = halves(value)
    start = value.shape[0]
    ref[0:start, :] = high
    ref[start : 2 * start, :] = low


def apply(stacked, right, rows):
    both = product(stacked[:, : right.shape[0]], right)
    start = stacked.shape[0] // 2
    return both[0:rows] + both[start : start + rows]


def apply_halves(stacked, right, rows):
    high, low = right
    start = stacked.shape[0] // 2
    rest = product(stacked[0:start, : low.shape[0]], low)
    return apply(stacked, high, rows) + rest[0:rows]


def lane_blocks(ref, start, count, across):
    return [ref[pl.ds(start + i, count, stride=across), :] for i in range(across)]


def rest_rows(count):
    return rounded(count, 8)


def rest_of(value, head, count):
    piece = value[head:]
    row = lax.broadcasted_iota(jnp.int32, piece.shape, 0)
    return jnp.where(row < count - head, piece, 0.0)


def stacked_rests(pieces, head):
    used = sum(piece.shape[0] for piece in pieces)
    return jnp.concatenate(list(pieces) + [jnp.zeros((head - used, pieces[0].shape[1]), F32)], axis=0)


def chunks(rows):
    return 2 if rows % 32 == 0 else 1


def start_copies(source, target, sems, first=0):
    rows = source.shape[0]
    size = rows // chunks(rows)
    copies = []
    for at in range(chunks(rows)):
        window = pl.ds(at * size, size)
        copies.append(pltpu.make_async_copy(source.at[window], target.at[window], sems.at[first + at]))
        copies[-1].start()
    return copies


def select_block(main, tail, firsts, which, rows, patterns, staged):
    staged[:, 0 : tail.shape[-1]] = tail[pl.ds(firsts[1] + which, rows, stride=patterns), :]
    return jnp.concatenate([main[pl.ds(firsts[0] + which, rows, stride=patterns), :], staged[...]], axis=1)


def pack_kernel(
    bands, count, across, prev, pattern_far, live_far, faces, inverses,
    kept, face_even, face_odd, side_even, side_odd, first, inverse_maps, upstream_maps, masks,
    wide, rows_even, rows_odd, main, tail, inverse_main, inverse_tail, staged, pattern, live, sems,
):
    along = prev.shape[-1]
    rows = prev.shape[0]
    copies = start_copies(prev, kept, sems)
    room, patterns, lanes = main.shape
    ragged = count - lanes
    small = [
        pltpu.make_async_copy(pattern_far, pattern, sems.at[2]),
        pltpu.make_async_copy(live_far, live, sems.at[3]),
    ]
    large = [
        pltpu.make_async_copy(
            inverses.at[:, :, pl.ds(0, lanes)], inverse_main.at[pl.ds(0, count)], sems.at[4]
        ),
        pltpu.make_async_copy(
            inverses.at[:, :, pl.ds(lanes, ragged)], inverse_tail.at[pl.ds(0, count)], sems.at[5]
        ),
        pltpu.make_async_copy(faces.at[0, :, :, pl.ds(0, lanes)], main.at[pl.ds(0, count)], sems.at[6]),
        pltpu.make_async_copy(faces.at[0, :, :, pl.ds(lanes, ragged)], tail.at[pl.ds(0, count)], sems.at[7]),
    ]
    for copy in small + large:
        copy.start()
    staged[...] = jnp.zeros(staged.shape, F32)
    wide[rows:, :] = jnp.zeros((wide.shape[0] - rows, along), F32)
    odd_x = lax.axis_index("cx") % 2 == 1
    odd_y = lax.axis_index("cy") % 2 == 1
    row = lax.broadcasted_iota(jnp.int32, (8, along), 0)
    lane = lax.broadcasted_iota(jnp.int32, (8, along), 1)
    last = along - 1
    even_lane, odd_lane = jnp.where(odd_y, 0, last), jnp.where(odd_y, last, 0)
    chosen = jnp.where(row == 0, even_lane, odd_lane)
    pick = jnp.where(lane == chosen, 1.0, 0.0).astype(BF16)
    size = rows // len(copies)
    done = 0
    for z in range(bands):
        while done * size < min(rows, ((z + 1) * count + 8) * across):
            copies[done].wait()
            window = pl.ds(done * size, size)
            wide[window, :] = kept[window, :].astype(F32)
            done += 1
        blocks = lane_blocks(wide, z * count * across, rest_rows(count), across)
        low, high = blocks[0], blocks[-1]
        face_even[z] = jnp.where(odd_x, low, high).astype(BF16)
        face_odd[z] = jnp.where(odd_x, high, low).astype(BF16)
        for i in range(across):
            found = lax.dot_general(
                pick, blocks[i][0:count].astype(BF16), (((1,), (1,)), ((), ())), preferred_element_type=F32
            )
            at = z * across + i
            rows_even[at : at + 1, :] = found[0:1]
            rows_odd[at : at + 1, :] = found[1:2]
    first[...] = kept[0 : count * across, :]
    side_even[...] = rows_even[...].astype(BF16)
    side_odd[...] = rows_odd[...].astype(BF16)
    for copy in small:
        copy.wait()
    slot = lax.broadcasted_iota(jnp.int32, (1, masks.shape[-1]), 1)
    counts = [live[z] for z in range(bands)]
    before, after = counts[0], counts[bands - 1]
    for z in range(bands):
        before = jnp.minimum(before, counts[z])
        after = jnp.minimum(after, counts[bands - 1 - z])
        for row, limit in ((z, counts[z]), (2 * bands - 1 - z, after), (2 * bands + z, before)):
            masks[row : row + 1, :] = jnp.where(slot < limit, 1.0, 0.0)
    for copy in large:
        copy.wait()
    high_rows = padded_rows(count)
    views = [
        (inverse_main.reshape(room * patterns, lanes), inverse_tail.reshape(room * patterns, ragged), inverse_maps),
        (main.reshape(room * patterns, lanes), tail.reshape(room * patterns, ragged), upstream_maps),
    ]
    for at, (near, rest, target) in enumerate(views):
        for z in range(bands):
            value = select_block(near, rest, (0, 0), pattern[z], high_rows, patterns, staged.at[at * bands + z])
            store_halves(target.at[z], value)


def parts(ref, count):
    start = ref.shape[0] // 2
    return ref[0:count, :], ref[start : start + count, :]


def combine(out, left, right, count):
    store_halves(out, apply_halves(left[...], parts(right, count), out.shape[0] // 2))


def matrix_kernel(
    bands, count, pattern_far, faces, right, inverse_maps, upstream_maps,
    right_kept, maps, step_maps, reach, chains,
    main, tail, pool, staged, pattern, sems,
):
    patterns, lanes = main.shape[1:]
    ragged = count - lanes
    high_rows = padded_rows(count)
    room = tail.shape[1]
    used = tail.shape[0]
    copies = [pltpu.make_async_copy(pattern_far, pattern, sems.at[0])]
    for at in range(used):
        source = faces.at[at + 1]
        copies.append(
            pltpu.make_async_copy(
                source.at[:, :, pl.ds(0, lanes)], main.at[pl.ds(at * count, count)], sems.at[1 + 2 * at]
            )
        )
        copies.append(
            pltpu.make_async_copy(
                source.at[:, :, pl.ds(lanes, ragged)], tail.at[at, pl.ds(0, count)], sems.at[2 + 2 * at]
            )
        )
    copies.append(pltpu.make_async_copy(right, right_kept, sems.at[1 + 2 * used]))
    for copy in copies:
        copy.start()
    staged[...] = jnp.zeros(staged.shape, F32)
    main_rows = main.reshape(main.shape[0] * patterns, lanes)
    tail_rows = tail.reshape(used * room * patterns, ragged)

    def selected(band, face):
        at = face - 1
        firsts = (at * count * patterns, at * room * patterns)
        return select_block(
            main_rows, tail_rows, firsts, pattern[band], high_rows, patterns, staged.at[at * bands + band]
        )

    for z in range(bands):
        upstream = parts(upstream_maps.at[z], count)
        store_halves(step_maps.at[z], -apply_halves(inverse_maps[z], upstream, high_rows))
    spare = [0]

    def fresh():
        spare[0] += 1
        return pool.at[spare[0] - 1]

    def solve(low, high, top):
        if high - low == 1:
            return {low: inverse_maps.at[low]}, step_maps.at[low]
        middle = (low + high) // 2
        near, near_step = solve(low, middle, False)
        found, far_step = solve(middle, high, False)
        for z, ref in near.items():
            found[z] = fresh()
            combine(found[z], far_step, ref, count)
        step = None
        if not top:
            step = fresh()
            combine(step, far_step, near_step, count)
        return found, step

    full_reach, _ = solve(0, bands, True)
    chains[0] = step_maps[0]
    for z in range(1, bands):
        combine(chains.at[z], step_maps.at[z], chains.at[z - 1], count)

    def put(ref, tile, value):
        high, low = halves(value)
        window = pl.ds(tile * lanes, lanes)
        ref[0:high_rows, window] = high
        ref[high_rows : 2 * high_rows, window] = low

    rests = [None] * bands
    total = maps.shape[2] // lanes - 1

    copies[0].wait()

    def take(face):
        for copy in copies[2 * face - 1 : 2 * face + 1]:
            copy.wait()
        for z in range(bands):
            value = selected(z, face)
            put(maps.at[z], face - 1, value[:, :lanes])
            rest = pltpu.roll(value[:, lanes:], 8 * (face - 1), axis=1)
            rests[z] = rest if rests[z] is None else rests[z] + rest

    reach_rest = None
    for z in range(bands):
        natural = full_reach[z]
        reach[:, pl.ds(z * lanes, lanes)] = natural[:, 0:lanes]
        rest = natural[0:high_rows, lanes:].astype(F32) + natural[high_rows:, lanes:].astype(F32)
        rest = pltpu.roll(rest, 8 * z, axis=1)
        reach_rest = rest if reach_rest is None else reach_rest + rest
    put(reach, bands, reach_rest)
    for face in range(1, used + 1):
        take(face)
    for z in range(bands):
        put(maps.at[z], total, rests[z])
    copies[-1].wait()


def local_kernel(
    bands, count, across, right, prev, follow, side_even, side_odd, face_even, face_odd, maps, reach, masks,
    base, last_band, heads, rests, wide, wide_right, wide_follow, sides, shifted, rest_stacks, high_stack, low_stack,
):
    rows, along = right.shape
    block = count * across
    deep = rest_rows(count)
    head = count // 128 * 128
    edge = (across - 1) * along
    odd_y = lax.axis_index("cy") % 2 == 1
    has_next = lax.axis_index("sweep") < lax.axis_size("sweep") - 1
    wide[0:rows, :] = prev[...].astype(F32)
    for z in range(bands):
        for i, value in enumerate(lane_blocks(wide, z * block, deep, across)):
            window = pl.ds(i * along, along)
            heads[z, :, window] = value[0:head].astype(BF16)
            rests[z, :, window] = rest_of(value, head, count)
    wide_right[0:rows, :] = right[...].astype(F32)
    wide_follow[0:block, :] = jnp.where(has_next, follow[...].astype(F32), 0.0)
    even, odd = side_even[...].astype(F32), without_wrap(side_odd[...].astype(F32), "cy")
    total = bands * across
    sides[0:total, 0:count] = jnp.where(odd_y, even, odd)
    sides[total : 2 * total, 0:count] = jnp.where(odd_y, odd, even)
    columns = sides[...].T
    lane = lax.broadcasted_iota(jnp.int32, (deep, along), 1)
    beyond = lane_blocks(wide_follow, 0, deep, across)
    beyond_head = jnp.concatenate([value[0:head].astype(BF16) for value in beyond], axis=1)
    beyond_rest = jnp.concatenate([rest_of(value, head, count) for value in beyond], axis=1)
    final_rests = []
    for z in range(bands):
        minus, plus = edges_of(face_even, face_odd, z)
        behind_rests, ahead_rests = [], []
        for i in range(across):
            window = slice(i * along, (i + 1) * along)
            value = jnp.concatenate([heads[z, :, window].astype(F32), rests[z, :, window]], axis=0)
            at = z * across + i
            column = columns[0:deep, at : at + 1]
            behind = jnp.where(lane == 0, column, pltpu.roll(value, 1, axis=1))
            column = columns[0:deep, at + total : at + total + 1]
            ahead = jnp.where(lane == along - 1, column, pltpu.roll(value, along - 1, axis=1))
            shifted[z, 0:head, window] = behind[0:head].astype(BF16)
            shifted[z, head:, window] = ahead[0:head].astype(BF16)
            behind_rests.append(rest_of(behind, head, count))
            ahead_rests.append(rest_of(ahead, head, count))
        own, own_rest = heads[z], rests[z]
        pieces = [
            rests[z + 1] if z + 1 < bands else beyond_rest,
            jnp.concatenate([rest_of(minus, head, count), own_rest[:, :edge]], axis=1),
            jnp.concatenate([own_rest[:, along:], rest_of(plus, head, count)], axis=1),
            jnp.concatenate(behind_rests, axis=1),
            jnp.concatenate(ahead_rests, axis=1),
        ]
        rest_stacks[z] = stacked_rests(pieces, head).astype(BF16)
        fields = jnp.concatenate(
            [
                heads[z + 1] if z + 1 < bands else beyond_head,
                jnp.concatenate([minus[0:head].astype(BF16), own[:, :edge]], axis=1),
                jnp.concatenate([own[:, along:], plus[0:head].astype(BF16)], axis=1),
                shifted[z],
                rest_stacks[z],
            ],
            axis=0,
        )
        drop = apply(maps[z], fields, deep)
        value = jnp.concatenate(lane_blocks(wide_right, z * block, deep, across), axis=1) - drop
        base[z] = value[0:count]
        value = value * masks[bands + z : bands + z + 1, :]
        high, low = halves(value[0:head])
        high_stack[z * head : (z + 1) * head, :] = high
        low_stack[z * head : (z + 1) * head, :] = low
        final_rests.append(rest_of(value, head, count))
    high, low = halves(stacked_rests(final_rests, head))
    high_stack[bands * head :, :] = high
    low_stack[bands * head :, :] = low
    last_band[...] = apply_halves(reach[...], (high_stack[...], low_stack[...]), count)


def without_wrap(value, axis):
    size = lax.axis_size(axis)
    if size % 2:
        return value
    index = lax.axis_index(axis)
    return jnp.where((index > 0) & (index < size - 1), value, 0.0)


def edges_of(face_even, face_odd, z):
    odd_x = lax.axis_index("cx") % 2 == 1
    even, odd = face_even[z].astype(F32), without_wrap(face_odd[z].astype(F32), "cx")
    return jnp.where(odd_x, even, odd), jnp.where(odd_x, odd, even)


def sweep_kernel(bands, count, base, masks, inverse_maps, step_maps, states):
    shares = [apply_halves(inverse_maps[z], halves(base[z]), count) for z in range(bands)]
    current = None
    for z in range(bands):
        value = shares[z]
        if z > 0:
            value = value + apply_halves(step_maps[z], halves(current), count)
        current = value * masks[z : z + 1, :]
        states[z] = current


def finish_kernel(bands, count, across, masks, states, chains, incoming, out, staged, sems):
    cells = incoming.shape[-1]
    along = cells // across
    rows = staged.shape[0]
    right = halves(jnp.where(lax.axis_index("sweep") > 0, incoming[...], 0.0))
    copies = []
    sent = 0
    for z in range(bands):
        moved = apply_halves(chains[z], right, count)
        value = states[z] + moved * masks[2 * bands + z : 2 * bands + z + 1, :]
        for i in range(across):
            staged[pl.ds(z * count * across + i, count, stride=across), :] = value[:, i * along : (i + 1) * along]
        ready = (z + 1) * count * across
        ready = rows if ready == rows else ready // 8 * 8
        window = pl.ds(sent, ready - sent)
        copies.append(pltpu.make_async_copy(staged.at[window], out.at[window], sems.at[z]))
        copies[-1].start()
        sent = ready
    for copy in copies:
        copy.wait()


def call(kernel, out, specs, scratch=(), flops=0, moved=0, out_specs=None):
    return pl.pallas_call(
        kernel,
        out_shape=out,
        in_specs=specs,
        out_specs=out_specs or jax.tree.map(lambda _: VMEM, out),
        scratch_shapes=scratch,
        cost_estimate=pl.CostEstimate(flops=flops, bytes_accessed=moved, transcendentals=0),
        compiler_params=pltpu.CompilerParams(vmem_limit_bytes=32 * 2**20),
    )


def in_hbm(value):
    return pltpu.with_memory_space_constraint(value, pltpu.HBM)


def swapped(value, axis, first):
    size = lax.axis_size(axis)
    pairs = []
    for left in range(first, size - 1 + first * (1 - size % 2), 2):
        right = (left + 1) % size
        pairs += [(left, right), (right, left)]
    return lax.ppermute(value, axis, pairs)


def passed_along(value, axis, steps):
    count = lax.axis_size(axis)
    if count == 2:
        return swapped(value, axis, 0)
    first, last = (max(0, -steps), min(count, count - steps))
    return lax.ppermute(value, axis, [(source, source + steps) for source in range(first, last)])


def on_device(right_side, previous, diag_inverse, face_blocks, pattern, live_count):
    bands, count, across, along = right_side.shape
    cells, rows = across * along, bands * count * across
    pads, wide_count = 2 * padded_rows(count), rounded(count, 128)
    shape = jax.ShapeDtypeStruct
    patterns, face_total = face_blocks.shape[:2]
    lanes = count // 128 * 128
    right = in_hbm(right_side.reshape(rows, along))
    prev = in_hbm(previous.reshape(rows, along))
    faces = in_hbm(face_blocks.transpose(1, 2, 0, 3))
    inverses = in_hbm(diag_inverse.transpose(1, 0, 2))
    live = in_hbm(live_count.reshape(bands))
    pattern = in_hbm(pattern)
    deep = rest_rows(count)
    face = shape((bands, deep, along), BF16)
    side = shape((bands * across, count), BF16)
    field = shape((rows, along), BF16)
    side_rows = pltpu.VMEM((bands * across, count), F32)
    filled = pltpu.VMEM((rows + 8 * across, along), F32)
    wide = pltpu.VMEM((rows, along), F32)
    matrix = shape((bands, pads, wide_count), BF16)
    block_room = [
        pltpu.VMEM((count + 16, patterns, lanes), F32),
        pltpu.VMEM((count + 16, patterns, count - lanes), F32),
    ]
    small_room = pltpu.SMEM((bands,), jnp.int32)
    (
        kept, face_even, face_odd, side_even, side_odd, first, inverse_maps, upstream_maps, masks
    ) = call(
        functools.partial(pack_kernel, bands, count, across),
        (
            field,
            face,
            face,
            side,
            side,
            shape((count * across, along), BF16),
            matrix,
            matrix,
            shape((3 * bands, cells), F32),
        ),
        [HBM] * 5,
        [filled, side_rows, side_rows]
        + block_room * 2
        + [pltpu.VMEM((2 * bands, pads // 2, lanes), F32), small_room, small_room, pltpu.SemaphoreType.DMA((8,))],
        moved=rows * along * 4,
    )(prev, pattern, live, faces, inverses)
    side_even = swapped(side_even, "cy", 0)
    side_odd = swapped(side_odd, "cy", 1)
    follow = passed_along(first, "sweep", -1)
    face_odd = swapped(face_odd, "cx", 1)
    face_even = swapped(face_even, "cx", 0)
    step_flops = count * count * cells * 2
    used = face_total - 1
    right_kept, maps, step_maps, reach, chains = call(
        functools.partial(matrix_kernel, bands, count),
        (
            field,
            shape((bands, pads, face_total * lanes), BF16),
            matrix,
            shape((pads, (bands + 1) * lanes), BF16),
            matrix,
        ),
        [HBM, HBM, HBM, VMEM, VMEM],
        [
            pltpu.VMEM((used * count + 16, patterns, lanes), F32),
            pltpu.VMEM((used, count + 16, patterns, count - lanes), F32),
            pltpu.VMEM((4 * bands, pads, wide_count), BF16),
            pltpu.VMEM((used * bands, pads // 2, lanes), F32),
            small_room,
            pltpu.SemaphoreType.DMA((2 * used + 2,)),
        ],
        flops=bands * 5 * step_flops,
        moved=4 * 2**20,
    )(pattern, faces, right, inverse_maps, upstream_maps)
    base, last = call(
        functools.partial(local_kernel, bands, count, across),
        (shape((bands, count, cells), F32), shape((count, cells), F32)),
        [VMEM] * 10,
        [
            pltpu.VMEM((bands, lanes, cells), BF16),
            pltpu.VMEM((bands, deep - lanes, cells), F32),
            filled,
            filled,
            pltpu.VMEM(((count + 8) * across, along), F32),
            pltpu.VMEM((rounded(2 * bands * across, 128), rounded(count, 128)), F32),
            pltpu.VMEM((bands, 2 * lanes, cells), BF16),
            pltpu.VMEM((bands, lanes, cells), BF16),
            pltpu.VMEM(((bands + 1) * lanes, cells), BF16),
            pltpu.VMEM(((bands + 1) * lanes, cells), BF16),
        ],
        flops=bands * 13 * step_flops,
        moved=2**20,
    )(right_kept, kept, follow, side_even, side_odd, face_even, face_odd, maps, reach, masks)
    states = call(
        functools.partial(sweep_kernel, bands, count),
        shape((bands, count, cells), F32),
        [VMEM] * 4,
        flops=bands * 7 * step_flops,
        moved=2**20,
    )(base, masks, inverse_maps, step_maps)
    incoming = passed_along(last, "sweep", 1)
    if lax.axis_size("sweep") > 2:
        start = padded_rows(count)
        end_map = chains[-1, 0:count, 0:count].astype(F32) + chains[-1, start : start + count, 0:count].astype(F32)
        slot = jnp.arange(cells, dtype=jnp.int32)
        kept = (slot < jnp.min(live_count)).astype(F32)

        def relay(_, arriving):
            product = jnp.dot(end_map, arriving, precision=lax.Precision.HIGHEST)
            return passed_along(last + kept[None, :] * product, "sweep", 1)

        incoming = lax.fori_loop(0, lax.axis_size("sweep") - 2, relay, incoming)
    out = call(
        functools.partial(finish_kernel, bands, count, across),
        shape((rows, along), F32),
        [VMEM] * 4,
        [wide, pltpu.SemaphoreType.DMA((bands,))],
        flops=bands * 3 * step_flops,
        moved=2**20,
        out_specs=HBM,
    )(masks, states, chains, incoming)
    return out.reshape(bands, count, across, along)


def solution(mesh):
    return jax.shard_map(
        on_device,
        mesh=mesh,
        in_specs=(
            P("sweep", None, "cx", "cy"),
            P("sweep", None, "cx", "cy"),
            P(),
            P(),
            P("sweep"),
            P("sweep", "cx", "cy"),
        ),
        out_specs=P("sweep", None, "cx", "cy"),
        check_vma=False,
    )
```

```python
import functools

import jax
import jax.numpy as jnp
from jax import lax
from jax.experimental import pallas as pl
from jax.experimental.pallas import tpu as pltpu
from jax.sharding import PartitionSpec as P


F32, BF16 = jnp.float32, jnp.bfloat16
VMEM = pl.BlockSpec(memory_space=pltpu.VMEM)
HBM = pl.BlockSpec(memory_space=pltpu.HBM)


def rounded(count, unit):
    return (count + unit - 1) // unit * unit


def padded_rows(count):
    return rounded(count, 16)


def product(left, right):
    return jnp.dot(left, right, preferred_element_type=F32)


def halves(value):
    high = value.astype(BF16)
    return high, (value - high.astype(F32)).astype(BF16)


def store_halves(ref, value):
    high, low = halves(value)
    start = value.shape[0]
    ref[0:start, :] = high
    ref[start : 2 * start, :] = low


def apply(stacked, right, rows):
    both = product(stacked[:, : right.shape[0]], right)
    start = stacked.shape[0] // 2
    return both[0:rows] + both[start : start + rows]


def apply_halves(stacked, right, rows):
    high, low = right
    start = stacked.shape[0] // 2
    rest = product(stacked[0:start, : low.shape[0]], low)
    return apply(stacked, high, rows) + rest[0:rows]


def lane_blocks(ref, start, count, across):
    return [ref[pl.ds(start + i, count, stride=across), :] for i in range(across)]


def rest_rows(count):
    return rounded(count, 8)


def rest_of(value, head, count):
    piece = value[head:]
    row = lax.broadcasted_iota(jnp.int32, piece.shape, 0)
    return jnp.where(row < count - head, piece, 0.0)


def stacked_rests(pieces, head):
    used = sum(piece.shape[0] for piece in pieces)
    return jnp.concatenate(list(pieces) + [jnp.zeros((head - used, pieces[0].shape[1]), F32)], axis=0)


def chunks(rows):
    return 2 if rows % 32 == 0 else 1


def start_copies(source, target, sems, first=0):
    rows = source.shape[0]
    size = rows // chunks(rows)
    copies = []
    for at in range(chunks(rows)):
        window = pl.ds(at * size, size)
        copies.append(pltpu.make_async_copy(source.at[window], target.at[window], sems.at[first + at]))
        copies[-1].start()
    return copies


def select_block(main, tail, firsts, which, rows, patterns, staged):
    staged[:, 0 : tail.shape[-1]] = tail[pl.ds(firsts[1] + which, rows, stride=patterns), :]
    return jnp.concatenate([main[pl.ds(firsts[0] + which, rows, stride=patterns), :], staged[...]], axis=1)


def pack_kernel(
    bands, count, across, prev, pattern_far, live_far, faces, inverses,
    kept, face_up, face_down, side_up, side_down, first, inverse_maps, upstream_maps, masks,
    wide, rows_up, rows_down, main, tail, inverse_main, inverse_tail, staged, pattern, live, sems,
):
    along = prev.shape[-1]
    rows = prev.shape[0]
    copies = start_copies(prev, kept, sems)
    room, patterns, lanes = main.shape
    ragged = count - lanes
    small = [
        pltpu.make_async_copy(pattern_far, pattern, sems.at[2]),
        pltpu.make_async_copy(live_far, live, sems.at[3]),
    ]
    large = [
        pltpu.make_async_copy(
            inverses.at[:, :, pl.ds(0, lanes)], inverse_main.at[pl.ds(0, count)], sems.at[4]
        ),
        pltpu.make_async_copy(
            inverses.at[:, :, pl.ds(lanes, ragged)], inverse_tail.at[pl.ds(0, count)], sems.at[5]
        ),
        pltpu.make_async_copy(faces.at[0, :, :, pl.ds(0, lanes)], main.at[pl.ds(0, count)], sems.at[6]),
        pltpu.make_async_copy(faces.at[0, :, :, pl.ds(lanes, ragged)], tail.at[pl.ds(0, count)], sems.at[7]),
    ]
    for copy in small + large:
        copy.start()
    staged[...] = jnp.zeros(staged.shape, F32)
    wide[rows:, :] = jnp.zeros((wide.shape[0] - rows, along), F32)
    row = lax.broadcasted_iota(jnp.int32, (8, along), 0)
    lane = lax.broadcasted_iota(jnp.int32, (8, along), 1)
    chosen = jnp.where(row == 0, along - 1, 0)
    pick = jnp.where(lane == chosen, 1.0, 0.0).astype(BF16)
    size = rows // len(copies)
    done = 0
    for z in range(bands):
        while done * size < min(rows, ((z + 1) * count + 8) * across):
            copies[done].wait()
            window = pl.ds(done * size, size)
            wide[window, :] = kept[window, :].astype(F32)
            done += 1
        blocks = lane_blocks(wide, z * count * across, rest_rows(count), across)
        low, high = blocks[0], blocks[-1]
        face_up[z] = high.astype(BF16)
        face_down[z] = low.astype(BF16)
        for i in range(across):
            found = lax.dot_general(
                pick, blocks[i][0:count].astype(BF16), (((1,), (1,)), ((), ())), preferred_element_type=F32
            )
            at = z * across + i
            rows_up[at : at + 1, :] = found[0:1]
            rows_down[at : at + 1, :] = found[1:2]
    first[...] = kept[0 : count * across, :]
    side_up[...] = rows_up[...].astype(BF16)
    side_down[...] = rows_down[...].astype(BF16)
    for copy in small:
        copy.wait()
    slot = lax.broadcasted_iota(jnp.int32, (1, masks.shape[-1]), 1)
    counts = [live[z] for z in range(bands)]
    before, after = counts[0], counts[bands - 1]
    for z in range(bands):
        before = jnp.minimum(before, counts[z])
        after = jnp.minimum(after, counts[bands - 1 - z])
        for row, limit in ((z, counts[z]), (2 * bands - 1 - z, after), (2 * bands + z, before)):
            masks[row : row + 1, :] = jnp.where(slot < limit, 1.0, 0.0)
    for copy in large:
        copy.wait()
    high_rows = padded_rows(count)
    views = [
        (inverse_main.reshape(room * patterns, lanes), inverse_tail.reshape(room * patterns, ragged), inverse_maps),
        (main.reshape(room * patterns, lanes), tail.reshape(room * patterns, ragged), upstream_maps),
    ]
    for at, (near, rest, target) in enumerate(views):
        for z in range(bands):
            value = select_block(near, rest, (0, 0), pattern[z], high_rows, patterns, staged.at[at * bands + z])
            store_halves(target.at[z], value)


def parts(ref, count):
    start = ref.shape[0] // 2
    return ref[0:count, :], ref[start : start + count, :]


def combine(out, left, right, count):
    store_halves(out, apply_halves(left[...], parts(right, count), out.shape[0] // 2))


def matrix_kernel(
    bands, count, pattern_far, faces, right, inverse_maps, upstream_maps,
    right_kept, maps, step_maps, reach, chains,
    main, tail, pool, staged, pattern, sems,
):
    patterns, lanes = main.shape[1:]
    ragged = count - lanes
    high_rows = padded_rows(count)
    room = tail.shape[1]
    used = tail.shape[0]
    copies = [pltpu.make_async_copy(pattern_far, pattern, sems.at[0])]
    for at in range(used):
        source = faces.at[at + 1]
        copies.append(
            pltpu.make_async_copy(
                source.at[:, :, pl.ds(0, lanes)], main.at[pl.ds(at * count, count)], sems.at[1 + 2 * at]
            )
        )
        copies.append(
            pltpu.make_async_copy(
                source.at[:, :, pl.ds(lanes, ragged)], tail.at[at, pl.ds(0, count)], sems.at[2 + 2 * at]
            )
        )
    copies.append(pltpu.make_async_copy(right, right_kept, sems.at[1 + 2 * used]))
    for copy in copies:
        copy.start()
    staged[...] = jnp.zeros(staged.shape, F32)
    main_rows = main.reshape(main.shape[0] * patterns, lanes)
    tail_rows = tail.reshape(used * room * patterns, ragged)

    def selected(band, face):
        at = face - 1
        firsts = (at * count * patterns, at * room * patterns)
        return select_block(
            main_rows, tail_rows, firsts, pattern[band], high_rows, patterns, staged.at[at * bands + band]
        )

    for z in range(bands):
        upstream = parts(upstream_maps.at[z], count)
        store_halves(step_maps.at[z], -apply_halves(inverse_maps[z], upstream, high_rows))
    spare = [0]

    def fresh():
        spare[0] += 1
        return pool.at[spare[0] - 1]

    def solve(low, high, top):
        if high - low == 1:
            return {low: inverse_maps.at[low]}, step_maps.at[low]
        middle = (low + high) // 2
        near, near_step = solve(low, middle, False)
        found, far_step = solve(middle, high, False)
        for z, ref in near.items():
            found[z] = fresh()
            combine(found[z], far_step, ref, count)
        step = None
        if not top:
            step = fresh()
            combine(step, far_step, near_step, count)
        return found, step

    full_reach, _ = solve(0, bands, True)
    chains[0] = step_maps[0]
    for z in range(1, bands):
        combine(chains.at[z], step_maps.at[z], chains.at[z - 1], count)

    def put(ref, tile, value):
        high, low = halves(value)
        window = pl.ds(tile * lanes, lanes)
        ref[0:high_rows, window] = high
        ref[high_rows : 2 * high_rows, window] = low

    rests = [None] * bands
    total = maps.shape[2] // lanes - 1

    copies[0].wait()

    def take(face):
        for copy in copies[2 * face - 1 : 2 * face + 1]:
            copy.wait()
        for z in range(bands):
            value = selected(z, face)
            put(maps.at[z], face - 1, value[:, :lanes])
            rest = pltpu.roll(value[:, lanes:], 8 * (face - 1), axis=1)
            rests[z] = rest if rests[z] is None else rests[z] + rest

    reach_rest = None
    for z in range(bands):
        natural = full_reach[z]
        reach[:, pl.ds(z * lanes, lanes)] = natural[:, 0:lanes]
        rest = natural[0:high_rows, lanes:].astype(F32) + natural[high_rows:, lanes:].astype(F32)
        rest = pltpu.roll(rest, 8 * z, axis=1)
        reach_rest = rest if reach_rest is None else reach_rest + rest
    put(reach, bands, reach_rest)
    for face in range(1, used + 1):
        take(face)
    for z in range(bands):
        put(maps.at[z], total, rests[z])
    copies[-1].wait()


def local_kernel(
    bands, count, across, right, prev, follow, side_up, side_down, face_up, face_down, maps, reach, masks,
    base, last_band, heads, rests, wide, wide_right, wide_follow, sides, shifted, rest_stacks, high_stack, low_stack,
):
    rows, along = right.shape
    block = count * across
    deep = rest_rows(count)
    head = count // 128 * 128
    edge = (across - 1) * along
    has_next = lax.axis_index("sweep") < lax.axis_size("sweep") - 1
    wide[0:rows, :] = prev[...].astype(F32)
    for z in range(bands):
        for i, value in enumerate(lane_blocks(wide, z * block, deep, across)):
            window = pl.ds(i * along, along)
            heads[z, :, window] = value[0:head].astype(BF16)
            rests[z, :, window] = rest_of(value, head, count)
    wide_right[0:rows, :] = right[...].astype(F32)
    wide_follow[0:block, :] = jnp.where(has_next, follow[...].astype(F32), 0.0)
    minus, plus = between(side_up[...], side_down[...], "cy")
    total = bands * across
    sides[0:total, 0:count] = minus
    sides[total : 2 * total, 0:count] = plus
    columns = sides[...].T
    lane = lax.broadcasted_iota(jnp.int32, (deep, along), 1)
    beyond = lane_blocks(wide_follow, 0, deep, across)
    beyond_head = jnp.concatenate([value[0:head].astype(BF16) for value in beyond], axis=1)
    beyond_rest = jnp.concatenate([rest_of(value, head, count) for value in beyond], axis=1)
    final_rests = []
    for z in range(bands):
        minus, plus = between(face_up[z], face_down[z], "cx")
        behind_rests, ahead_rests = [], []
        for i in range(across):
            window = slice(i * along, (i + 1) * along)
            value = jnp.concatenate([heads[z, :, window].astype(F32), rests[z, :, window]], axis=0)
            at = z * across + i
            column = columns[0:deep, at : at + 1]
            behind = jnp.where(lane == 0, column, pltpu.roll(value, 1, axis=1))
            column = columns[0:deep, at + total : at + total + 1]
            ahead = jnp.where(lane == along - 1, column, pltpu.roll(value, along - 1, axis=1))
            shifted[z, 0:head, window] = behind[0:head].astype(BF16)
            shifted[z, head:, window] = ahead[0:head].astype(BF16)
            behind_rests.append(rest_of(behind, head, count))
            ahead_rests.append(rest_of(ahead, head, count))
        own, own_rest = heads[z], rests[z]
        pieces = [
            rests[z + 1] if z + 1 < bands else beyond_rest,
            jnp.concatenate([rest_of(minus, head, count), own_rest[:, :edge]], axis=1),
            jnp.concatenate([own_rest[:, along:], rest_of(plus, head, count)], axis=1),
            jnp.concatenate(behind_rests, axis=1),
            jnp.concatenate(ahead_rests, axis=1),
        ]
        rest_stacks[z] = stacked_rests(pieces, head).astype(BF16)
        fields = jnp.concatenate(
            [
                heads[z + 1] if z + 1 < bands else beyond_head,
                jnp.concatenate([minus[0:head].astype(BF16), own[:, :edge]], axis=1),
                jnp.concatenate([own[:, along:], plus[0:head].astype(BF16)], axis=1),
                shifted[z],
                rest_stacks[z],
            ],
            axis=0,
        )
        drop = apply(maps[z], fields, deep)
        value = jnp.concatenate(lane_blocks(wide_right, z * block, deep, across), axis=1) - drop
        base[z] = value[0:count]
        value = value * masks[bands + z : bands + z + 1, :]
        high, low = halves(value[0:head])
        high_stack[z * head : (z + 1) * head, :] = high
        low_stack[z * head : (z + 1) * head, :] = low
        final_rests.append(rest_of(value, head, count))
    high, low = halves(stacked_rests(final_rests, head))
    high_stack[bands * head :, :] = high
    low_stack[bands * head :, :] = low
    last_band[...] = apply_halves(reach[...], (high_stack[...], low_stack[...]), count)


def between(upward, downward, axis):
    index = lax.axis_index(axis)
    minus = jnp.where(index > 0, upward.astype(F32), 0.0)
    return minus, jnp.where(index < lax.axis_size(axis) - 1, downward.astype(F32), 0.0)


def sweep_kernel(bands, count, base, masks, inverse_maps, step_maps, states):
    shares = [apply_halves(inverse_maps[z], halves(base[z]), count) for z in range(bands)]
    current = None
    for z in range(bands):
        value = shares[z]
        if z > 0:
            value = value + apply_halves(step_maps[z], halves(current), count)
        current = value * masks[z : z + 1, :]
        states[z] = current


def finish_kernel(bands, count, across, masks, states, chains, incoming, out, staged, sems):
    cells = incoming.shape[-1]
    along = cells // across
    rows = staged.shape[0]
    right = halves(jnp.where(lax.axis_index("sweep") > 0, incoming[...], 0.0))
    copies = []
    sent = 0
    for z in range(bands):
        moved = apply_halves(chains[z], right, count)
        value = states[z] + moved * masks[2 * bands + z : 2 * bands + z + 1, :]
        for i in range(across):
            staged[pl.ds(z * count * across + i, count, stride=across), :] = value[:, i * along : (i + 1) * along]
        ready = (z + 1) * count * across
        ready = rows if ready == rows else ready // 8 * 8
        window = pl.ds(sent, ready - sent)
        copies.append(pltpu.make_async_copy(staged.at[window], out.at[window], sems.at[z]))
        copies[-1].start()
        sent = ready
    for copy in copies:
        copy.wait()


def call(kernel, out, specs, scratch=(), flops=0, moved=0, out_specs=None):
    return pl.pallas_call(
        kernel,
        out_shape=out,
        in_specs=specs,
        out_specs=out_specs or jax.tree.map(lambda _: VMEM, out),
        scratch_shapes=scratch,
        cost_estimate=pl.CostEstimate(flops=flops, bytes_accessed=moved, transcendentals=0),
        compiler_params=pltpu.CompilerParams(vmem_limit_bytes=32 * 2**20),
    )


def in_hbm(value):
    return pltpu.with_memory_space_constraint(value, pltpu.HBM)


def around(value, axis, steps):
    size = lax.axis_size(axis)
    return lax.ppermute(value, axis, [(i, (i + steps) % size) for i in range(size)])


def passed_along(value, axis, steps):
    count = lax.axis_size(axis)
    if count == 2:
        return around(value, axis, steps)
    first, last = (max(0, -steps), min(count, count - steps))
    return lax.ppermute(value, axis, [(source, source + steps) for source in range(first, last)])


def on_device(right_side, previous, diag_inverse, face_blocks, pattern, live_count):
    bands, count, across, along = right_side.shape
    cells, rows = across * along, bands * count * across
    pads, wide_count = 2 * padded_rows(count), rounded(count, 128)
    shape = jax.ShapeDtypeStruct
    patterns, face_total = face_blocks.shape[:2]
    lanes = count // 128 * 128
    right = in_hbm(right_side.reshape(rows, along))
    prev = in_hbm(previous.reshape(rows, along))
    faces = in_hbm(face_blocks.transpose(1, 2, 0, 3))
    inverses = in_hbm(diag_inverse.transpose(1, 0, 2))
    live = in_hbm(live_count.reshape(bands))
    pattern = in_hbm(pattern)
    deep = rest_rows(count)
    face = shape((bands, deep, along), BF16)
    side = shape((bands * across, count), BF16)
    field = shape((rows, along), BF16)
    side_rows = pltpu.VMEM((bands * across, count), F32)
    filled = pltpu.VMEM((rows + 8 * across, along), F32)
    wide = pltpu.VMEM((rows, along), F32)
    matrix = shape((bands, pads, wide_count), BF16)
    block_room = [
        pltpu.VMEM((count + 16, patterns, lanes), F32),
        pltpu.VMEM((count + 16, patterns, count - lanes), F32),
    ]
    small_room = pltpu.SMEM((bands,), jnp.int32)
    (
        kept, face_up, face_down, side_up, side_down, first, inverse_maps, upstream_maps, masks
    ) = call(
        functools.partial(pack_kernel, bands, count, across),
        (
            field,
            face,
            face,
            side,
            side,
            shape((count * across, along), BF16),
            matrix,
            matrix,
            shape((3 * bands, cells), F32),
        ),
        [HBM] * 5,
        [filled, side_rows, side_rows]
        + block_room * 2
        + [pltpu.VMEM((2 * bands, pads // 2, lanes), F32), small_room, small_room, pltpu.SemaphoreType.DMA((8,))],
        moved=rows * along * 4,
    )(prev, pattern, live, faces, inverses)
    side_up = around(side_up, "cy", 1)
    side_down = around(side_down, "cy", -1)
    follow = passed_along(first, "sweep", -1)
    face_down = around(face_down, "cx", -1)
    face_up = around(face_up, "cx", 1)
    step_flops = count * count * cells * 2
    used = face_total - 1
    right_kept, maps, step_maps, reach, chains = call(
        functools.partial(matrix_kernel, bands, count),
        (
            field,
            shape((bands, pads, face_total * lanes), BF16),
            matrix,
            shape((pads, (bands + 1) * lanes), BF16),
            matrix,
        ),
        [HBM, HBM, HBM, VMEM, VMEM],
        [
            pltpu.VMEM((used * count + 16, patterns, lanes), F32),
            pltpu.VMEM((used, count + 16, patterns, count - lanes), F32),
            pltpu.VMEM((4 * bands, pads, wide_count), BF16),
            pltpu.VMEM((used * bands, pads // 2, lanes), F32),
            small_room,
            pltpu.SemaphoreType.DMA((2 * used + 2,)),
        ],
        flops=bands * 5 * step_flops,
        moved=4 * 2**20,
    )(pattern, faces, right, inverse_maps, upstream_maps)
    base, last = call(
        functools.partial(local_kernel, bands, count, across),
        (shape((bands, count, cells), F32), shape((count, cells), F32)),
        [VMEM] * 10,
        [
            pltpu.VMEM((bands, lanes, cells), BF16),
            pltpu.VMEM((bands, deep - lanes, cells), F32),
            filled,
            filled,
            pltpu.VMEM(((count + 8) * across, along), F32),
            pltpu.VMEM((rounded(2 * bands * across, 128), rounded(count, 128)), F32),
            pltpu.VMEM((bands, 2 * lanes, cells), BF16),
            pltpu.VMEM((bands, lanes, cells), BF16),
            pltpu.VMEM(((bands + 1) * lanes, cells), BF16),
            pltpu.VMEM(((bands + 1) * lanes, cells), BF16),
        ],
        flops=bands * 13 * step_flops,
        moved=2**20,
    )(right_kept, kept, follow, side_up, side_down, face_up, face_down, maps, reach, masks)
    states = call(
        functools.partial(sweep_kernel, bands, count),
        shape((bands, count, cells), F32),
        [VMEM] * 4,
        flops=bands * 7 * step_flops,
        moved=2**20,
    )(base, masks, inverse_maps, step_maps)
    incoming = passed_along(last, "sweep", 1)
    if lax.axis_size("sweep") > 2:
        start = padded_rows(count)
        end_map = chains[-1, 0:count, 0:count].astype(F32) + chains[-1, start : start + count, 0:count].astype(F32)
        slot = jnp.arange(cells, dtype=jnp.int32)
        kept = (slot < jnp.min(live_count)).astype(F32)

        def relay(_, arriving):
            product = jnp.dot(end_map, arriving, precision=lax.Precision.HIGHEST)
            return passed_along(last + kept[None, :] * product, "sweep", 1)

        incoming = lax.fori_loop(0, lax.axis_size("sweep") - 2, relay, incoming)
    out = call(
        functools.partial(finish_kernel, bands, count, across),
        shape((rows, along), F32),
        [VMEM] * 4,
        [wide, pltpu.SemaphoreType.DMA((bands,))],
        flops=bands * 3 * step_flops,
        moved=2**20,
        out_specs=HBM,
    )(masks, states, chains, incoming)
    return out.reshape(bands, count, across, along)


def solution(mesh):
    return jax.shard_map(
        on_device,
        mesh=mesh,
        in_specs=(
            P("sweep", None, "cx", "cy"),
            P("sweep", None, "cx", "cy"),
            P(),
            P(),
            P("sweep"),
            P("sweep", "cx", "cy"),
        ),
        out_specs=P("sweep", None, "cx", "cy"),
        check_vma=False,
    )
```
